128 devices in a mesh: group: 4 (over z_hi, core), dev: 32 (over z_lo, y, x).
Axes of the slice: x: 4, y: 4, z: 4 (z_hi: 2, z_lo: 2; z = z_hi * 2 + z_lo), core: 2. Of those that a mesh axis runs over, the one named last changes fastest.
Arguments:
- velocity: float32 [3, 1024, 128, 128], P(None, ('group', 'dev')), may hold values from -3 to 3
- viscosity: float32 [1024, 128, 128], P(('group', 'dev')), may hold values from 0.04 to 0.3
- sample_idx: int32 [128, 256], P(('group', 'dev')), may hold values from 0 to 255, as said below
- assign: int32 [128, 256], P(('group', 'dev')), may hold values from 0 to 32767, as said below
- params: float32 [3670016], P(('group', 'dev')), may hold values from -0.15 to 0.15
- adam_m: float32 [3670016], P(('group', 'dev')), may hold values from -0.3 to 0.3
- adam_v: float32 [3670016], P(('group', 'dev')), may hold values from 0.0001 to 0.01
Outputs:
- velocity_next: float32 [3, 1024, 128, 128], P(None, ('group', 'dev'))
- prediction: float32 [32768, 1536], P(('group', 'dev'))
- new_params: float32 [3670016], P(('group', 'dev'))
- new_m: float32 [3670016], P(('group', 'dev'))
- new_v: float32 [3670016], P(('group', 'dev'))
The draws below stay inside these ranges and needn't reach their ends.
Inputs may be any that keep to these rules, and one draw needn't show every extreme that they name: `sample_idx`: each row holds 256 different patch numbers; 0 and the largest patch number appear in every row. `assign`: all entries together are a permutation of the 32768 learner slots; each row names exactly 2 slots of every block of 256 consecutive slots.
All inputs are finite; a program needn't handle non-finite values.
Results may differ from the reference program's by a relative error of at most 0.00011.
Values sent between devices are 32-bit elements; how exact they have to be, the bound alone decides.
A program may use at most 192 MiB of HBM per device.

```python
import math
import jax
import jax.numpy as jnp
from jax import lax

PATCH = 8
D = 512
H = 2048
NY = 128
NZ = 128
TOK_DEV = 256
CX = 8
NX = 1024
F = 1536
NPARAM = 3670016
TOKENS = 32768
N_GROUP = 4
N_DEV = 32


def draw_sample_idx(key, part):
    blocks = N_GROUP * N_DEV
    count = NY // PATCH * (NZ // PATCH)

    def one_row(row_key):
        pick_key, order_key = jax.random.split(row_key)
        middle = jax.random.permutation(pick_key, count - 2)[:TOK_DEV - 2].astype(jnp.int32) + 1
        row = jnp.concatenate([jnp.zeros((1,), jnp.int32), jnp.full((1,), count - 1, jnp.int32), middle])
        return jax.random.permutation(order_key, row).astype(jnp.int32)
    return jax.vmap(one_row)(jax.random.split(jax.random.fold_in(key, 11), blocks))


def draw_assign(key, part):
    blocks = N_GROUP * N_DEV
    per_peer = TOK_DEV // blocks
    base = jax.random.fold_in(key, 23)
    route_key, slot_key = jax.random.split(base)
    routes = jax.vmap(lambda k: jax.random.permutation(k, TOK_DEV))(jax.random.split(route_key, blocks)).astype(jnp.int32)
    places = jax.vmap(lambda k: jax.random.permutation(k, TOK_DEV))(jax.random.split(slot_key, blocks)).astype(jnp.int32)
    target = routes // per_peer
    within = routes % per_peer
    source = jnp.arange(blocks, dtype=jnp.int32)[:, None]
    return (target * TOK_DEV + places[target, source * per_peer + within]).astype(jnp.int32)


def shard_levels(rng, shape, pieces, smallest, top_value):
    def one(position, shards_of):
        draws = jax.random.uniform(jax.random.fold_in(jax.random.fold_in(rng, 6), position), (shards_of,), jnp.float32, smallest / len(pieces), top_value / len(pieces))
        return jnp.repeat(jnp.exp(draws), shape[position] // shards_of).reshape((-1,) + (1,) * (len(shape) - position - 1))

    loudness = one(*pieces[0])
    for cut in pieces[1:]:
        loudness = loudness * one(*cut)
    return loudness


def normal_values(rng, dims, width, reach, pieces=(), kind=jnp.bfloat16):
    values = width * jax.random.normal(rng, dims, jnp.float32)
    if pieces:
        values = values * shard_levels(rng, dims, pieces, -0.22, 0.18)
    return jnp.clip(values, -reach, reach).astype(kind)


def setup_inputs(seed: int = 0) -> dict:
    splits = jax.random.split(jax.random.key(seed), 8)
    velocity = normal_values(splits[0], (3, NX, NY, NZ), 0.5, 3.0, ((1, 128),), jnp.float32)
    viscosity = jnp.clip(jnp.exp(math.log(0.3) - 2.014903 * jax.random.uniform(splits[1], (NX, NY, NZ), jnp.float32) ** shard_levels(splits[1], (NX, NY, NZ), ((0, 128),), -0.2, 0.2)), 0.04, 0.3)
    sample_idx = draw_sample_idx(jax.random.fold_in(splits[7], 71), 0)
    assign = draw_assign(jax.random.fold_in(splits[7], 71), 0)
    params = normal_values(splits[4], (NPARAM,), 0.03, 0.15, ((0, 128),), jnp.float32)
    adam_m = normal_values(splits[5], (NPARAM,), 0.05, 0.3, ((0, 128),), jnp.float32)
    adam_v = jnp.clip(jnp.exp(math.log(0.01) - 4.6051702 * jax.random.uniform(splits[6], (NPARAM,), jnp.float32) ** shard_levels(splits[6], (NPARAM,), ((0, 128),), -0.2, 0.2)), 0.0001, 0.01)
    return {"velocity": velocity, "viscosity": viscosity, "sample_idx": sample_idx, "assign": assign, "params": params, "adam_m": adam_m, "adam_v": adam_v}


time_step = 0.5
norm_epsilon = 1e-06
beta_first = 0.9
beta_second = 0.95
learn_rate = 0.01
adam_epsilon = 1e-08
adam_count = 10

def advance(extended, visc_inner):
    centre = extended[:, 1:-1]
    upper_one = extended[:, 2:]
    lower_one = extended[:, :-2]
    upper_two = jnp.roll(centre, -1, 2)
    lower_two = jnp.roll(centre, 1, 2)
    upper_three = jnp.roll(centre, -1, 3)
    lower_three = jnp.roll(centre, 1, 3)
    laplace = upper_one + lower_one + upper_two + lower_two + upper_three + lower_three - 6.0 * centre
    advect = 0.5 * (centre[0:1] * (upper_one - lower_one) + centre[1:2] * (upper_two - lower_two) + centre[2:3] * (upper_three - lower_three))
    return centre + time_step * (visc_inner[None] * laplace - advect)

def patch_rows(block):
    depth = block.shape[1]
    span_y = block.shape[2] // depth
    span_z = block.shape[3] // depth
    tiles = block.reshape(3, depth, span_y, depth, span_z, depth).transpose(2, 4, 0, 1, 3, 5)
    return tiles.reshape(span_y * span_z, 3 * depth ** 3)

def matmul(left, right):
    return jnp.dot(left, right, precision=lax.Precision.HIGHEST, preferred_element_type=jnp.float32)

def forward(flat, inputs):
    first = F * D
    second = first + D * H
    third = second + H * D
    w_in = flat[:first].reshape(F, D)
    w_up = flat[first:second].reshape(D, H)
    w_down = flat[second:third].reshape(H, D)
    w_out = flat[third:].reshape(D, F)
    state = matmul(inputs, w_in)
    normed = state * lax.rsqrt(lax.optimization_barrier(jnp.mean(state * state, axis=-1, keepdims=True)) + norm_epsilon)
    hidden = jax.nn.gelu(matmul(normed, w_up), approximate=True)
    state = state + matmul(hidden, w_down)
    return inputs + matmul(state, w_out)

def batch_grad(flat, inputs, targets, count):

    def loss_fn(weights):
        guess = forward(weights, inputs)
        error = guess - targets
        return (0.5 * jnp.sum(error * error) / count, guess)
    loss, pull, guess = jax.vjp(loss_fn, flat, has_aux=True)
    grad, = pull(jnp.ones_like(loss))
    return (grad, guess)

def adam(shard, grad, moment, second):
    new_m = beta_first * moment + (1.0 - beta_first) * grad
    new_v = beta_second * second + (1.0 - beta_second) * grad * grad
    update = new_m / (1.0 - beta_first ** adam_count) / (jnp.sqrt(new_v / (1.0 - beta_second ** adam_count)) + adam_epsilon)
    return (shard - learn_rate * update, new_m, new_v)

def reference(velocity, viscosity, sample_idx, assign, params, adam_m, adam_v):
    blocks = N_GROUP * N_DEV
    padded_u = jnp.pad(velocity, ((0, 0), (2, 2), (0, 0), (0, 0)))
    padded_nu = jnp.pad(viscosity, ((2, 2), (0, 0), (0, 0)))

    def solve_block(item):
        index, rows = item
        start = index * CX
        extended = lax.dynamic_slice_in_dim(padded_u, start, CX + 4, 1)
        visc = lax.dynamic_slice_in_dim(padded_nu, start, CX + 4, 0)
        first = advance(extended, visc[1:-1])
        second = advance(first, visc[2:-2])
        current = first[:, 1:-1]
        return (second, patch_rows(current)[rows], patch_rows(second)[rows])
    stepped, tok_in, tok_out = lax.map(solve_block, (jnp.arange(blocks, dtype=jnp.int32), sample_idx))
    velocity_next = stepped.transpose(1, 0, 2, 3, 4).reshape(3, NX, NY, NZ)
    slots = assign.reshape(-1)
    inputs = jnp.zeros((TOKENS, F), jnp.float32).at[slots].set(tok_in.reshape(-1, F))
    targets = jnp.zeros((TOKENS, F), jnp.float32).at[slots].set(tok_out.reshape(-1, F))

    def learn(total, pair):
        grad, guess = batch_grad(params, pair[0], pair[1], TOK_DEV)
        return (total + grad, guess)
    grad, guesses = lax.scan(learn, jnp.zeros((NPARAM,), jnp.float32), (inputs.reshape(blocks, TOK_DEV, F), targets.reshape(blocks, TOK_DEV, F)))
    prediction = guesses.reshape(TOKENS, F)
    new_params, new_m, new_v = adam(params, grad, adam_m, adam_v)
    return (velocity_next, prediction, new_params, new_m, new_v)
```

```python
import jax
import jax.numpy as jnp
from jax import lax
from jax.experimental import pallas as pl
from jax.experimental.pallas import tpu as pltpu
from jax.sharding import PartitionSpec as P

time_step = 0.5
norm_epsilon = 1e-06
beta_first = 0.9
beta_second = 0.95
learn_rate = 0.01
adam_epsilon = 1e-08
adam_count = 10

MESH = pl.DeviceIdType.MESH
PIECES = ((0, 72), (72, 80), (152, 72))
GATHER = ((0, 72), (72, 80), (152, 80))
ORDERS = ((0, 1, 2), (1, 2, 0), (2, 0, 1))

def coords():
    g = lax.axis_index("group"); d = lax.axis_index("dev")
    return (d % 4, (d // 4) % 4, (g // 2) * 2 + d // 16), g % 2

def ident(xyz, core):
    x, y, z = xyz
    return ((z // 2) * 2 + core, (z % 2) * 16 + y * 4 + x)

def shifted(xyz, axis, by):
    out = list(xyz); out[axis] = (xyz[axis] + by) % 4
    return tuple(out)

def neighbours(xyz, core):
    ids = [ident(shifted(xyz, a, s), core) for a in range(3) for s in (1, 3)]
    return ids + [ident(xyz, 1 - core)]

def enter(xyz, core):
    barrier = pltpu.get_barrier_semaphore()
    ids = neighbours(xyz, core)
    for i in ids:
        pl.semaphore_signal(barrier, inc=1, device_id=i, device_id_type=MESH)
    pl.semaphore_wait(barrier, len(ids))

def region(ref, full, xyz, core, r0, n):
    x = slice(None) if 0 in full else xyz[0]
    y = slice(None) if 1 in full else xyz[1]
    zh = slice(None) if 2 in full else xyz[2] // 2
    zl = slice(None) if 2 in full else xyz[2] % 2
    return ref.at[zh, core, zl, y, x, pl.ds(r0, n), :]

def halves(piece, pieces=PIECES):
    r0, n = pieces[piece]
    n0 = (n // 16) * 8 if n % 16 else n // 2
    return (r0, n0), (r0 + n0, n - n0)

def ag_kernel(shard, out, lsem, ssem, rsem, cs, cr):
    xyz, core = coords()
    own = pltpu.make_async_copy(shard, out.at[xyz[2] // 2, core, xyz[2] % 2, xyz[1], xyz[0]], lsem)
    own.start()
    enter(xyz, core)
    own.wait()
    sib = ident(xyz, 1 - core)
    pend = []
    ncs = [0]
    sibs = []
    def send(src, slot, to):
        c = pltpu.make_async_remote_copy(src_ref=src, dst_ref=src, send_sem=ssem.at[slot], recv_sem=rsem.at[slot], device_id=to, device_id_type=MESH)
        c.start(); pend.append(c); return c
    def to_sib(src):
        k = ncs[0]; ncs[0] += 1
        c = pltpu.make_async_remote_copy(src_ref=src, dst_ref=src, send_sem=cs.at[k], recv_sem=cr.at[k], device_id=sib, device_id_type=MESH)
        c.start(); sibs.append(c)
    for phase in range(3):
        step1 = {}
        for p in range(3):
            a = ORDERS[p][phase]; full = ORDERS[p][:phase]
            R = ident(shifted(xyz, a, 1), core); L = ident(shifted(xyz, a, 3), core)
            (h0, n0), (h1, n1) = halves(p, GATHER)
            base = (phase * 3 + p) * 6
            step1[p, 0] = send(region(out, full, xyz, core, h0, n0), base + 0, R)
            step1[p, 3] = send(region(out, full, xyz, core, h1, n1), base + 3, L)
            step1[p, 1] = send(region(out, full, xyz, core, h1, n1), base + 1, R)
            step1[p, 4] = send(region(out, full, xyz, core, h0, n0), base + 4, L)
            if phase == 2:
                r0, n = GATHER[p]
                to_sib(region(out, full, xyz, core, r0, n))
        step2 = {}
        for p in range(3):
            a = ORDERS[p][phase]; full = ORDERS[p][:phase]
            R = ident(shifted(xyz, a, 1), core); L = ident(shifted(xyz, a, 3), core)
            left, right = shifted(xyz, a, 3), shifted(xyz, a, 1)
            (h0, n0), (h1, n1) = halves(p, GATHER)
            base = (phase * 3 + p) * 6
            step1[p, 0].wait_recv()
            step2[p, 2] = send(region(out, full, left, core, h0, n0), base + 2, R)
            step1[p, 3].wait_recv()
            step2[p, 5] = send(region(out, full, right, core, h1, n1), base + 5, L)
        for p in range(3):
            a = ORDERS[p][phase]; full = ORDERS[p][:phase]
            left, right, far = shifted(xyz, a, 3), shifted(xyz, a, 1), shifted(xyz, a, 2)
            step1[p, 1].wait_recv()
            step1[p, 4].wait_recv()
            r0, n = GATHER[p]
            if phase == 2:
                to_sib(region(out, full, left, core, r0, n))
                to_sib(region(out, full, right, core, r0, n))
        for p in range(3):
            a = ORDERS[p][phase]; full = ORDERS[p][:phase]
            far = shifted(xyz, a, 2)
            r0, n = GATHER[p]
            step2[p, 2].wait_recv()
            step2[p, 5].wait_recv()
            if phase == 2:
                to_sib(region(out, full, far, core, r0, n))
    for c in pend: c.wait_send()
    for c in sibs: c.wait_send()
    for c in sibs: c.wait_recv()

def all_gather(shard):
    return pl.pallas_call(
        ag_kernel,
        out_shape=jax.ShapeDtypeStruct((2, 2, 2, 4, 4, 232, 128), jnp.float32),
        in_specs=[pl.BlockSpec(memory_space=pl.ANY)],
        out_specs=pl.BlockSpec(memory_space=pl.ANY),
        scratch_shapes=[pltpu.SemaphoreType.DMA, pltpu.SemaphoreType.DMA((54,)), pltpu.SemaphoreType.DMA((54,)), pltpu.SemaphoreType.DMA((12,)), pltpu.SemaphoreType.DMA((12,))],
        compiler_params=pltpu.CompilerParams(collective_id=0, has_side_effects=True, vmem_limit_bytes=60 << 20),
        name="gather_params",
    )(shard)


def pick(full, xyz, present=(0, 1, 2)):
    out = []
    if 2 in present: out += [slice(None)] * 2 if 2 in full else [xyz[2] // 2, xyz[2] % 2]
    if 1 in present: out += [slice(None)] if 1 in full else [xyz[1]]
    if 0 in present: out += [slice(None)] if 0 in full else [xyz[0]]
    return tuple(out)

def walk(full, xyz, body):
    full = tuple(full)
    if not full:
        body(xyz); return
    def step(i, carry):
        at = list(xyz)
        for k, a in enumerate(full):
            at[a] = (i // (4 ** k)) % 4
        body(tuple(at)); return carry
    lax.fori_loop(0, 4 ** len(full), step, 0)

def dims(present):
    out = ()
    if 2 in present: out += (2, 2)
    if 1 in present: out += (4,)
    if 0 in present: out += (4,)
    return out

def rs_kernel(g, out, acc, crecv, *rest):
    bufs = {}; k = 0
    for phase in range(3):
        for p in range(3):
            for side in range(2):
                bufs[phase, p, side] = rest[k]; k += 1
    lsem, ssem, rsem, cs, cr = rest[k:]
    xyz, core = coords()
    load = [pltpu.make_async_copy(g.at[zh, core], acc.at[zh], lsem.at[zh]) for zh in range(2)]
    for c in load: c.start()
    enter(xyz, core)
    sib = ident(xyz, 1 - core)
    swaps = {}; pend = []
    for rel in (2, 1, 3, 0):
        for p in range(3):
            a = ORDERS[p][2]; full = ORDERS[p][:2]; r0, n = PIECES[p]
            at = shifted(xyz, a, rel); slot = len(swaps)
            i = pick(full, at)
            c = pltpu.make_async_remote_copy(src_ref=g.at[(i[0], 1 - core) + i[1:] + (pl.ds(r0, n),)], dst_ref=crecv.at[i + (pl.ds(r0, n),)],
                send_sem=cs.at[slot], recv_sem=cr.at[slot], device_id=sib, device_id_type=MESH)
            c.start(); swaps[p, rel] = c; pend.append(c)
    for c in load: c.wait()

    def swap_add(p, rel):
        a = ORDERS[p][2]; r0, n = PIECES[p]
        swaps[p, rel].wait_recv()
        def body(at):
            i = pick((), at) + (pl.ds(r0, n), slice(None))
            acc[i] = acc[i] + crecv[i]
        walk(ORDERS[p][:2], shifted(xyz, a, rel), body)

    for phase in range(3):
        def parts(p):
            a = ORDERS[p][2 - phase]; full = ORDERS[p][:2 - phase]; present = full + (a,)
            R = ident(shifted(xyz, a, 1), core); L = ident(shifted(xyz, a, 3), core)
            return a, full, present, R, L, halves(p), ((phase * 3 + p) * 6), PIECES[p][0]
        copies = {}
        def send(p, kind, rel, half, side):
            a, full, present, R, L, hs, base, start = parts(p)
            at = shifted(xyz, a, rel); r0, n = hs[half]
            c = pltpu.make_async_remote_copy(src_ref=acc.at[pick(full, at) + (pl.ds(r0, n),)],
                dst_ref=bufs[phase, p, side].at[pick(full, at, present) + (pl.ds(r0 - start, n),)],
                send_sem=ssem.at[base + kind], recv_sem=rsem.at[base + kind],
                device_id=(R, L)[side], device_id_type=MESH)
            c.start(); copies[p, kind] = c; pend.append(c)
        def fold(p, rel, half, side):
            a, full, present, R, L, hs, base, start = parts(p)
            buf = bufs[phase, p, side]; r0, n = hs[half]
            def body(at):
                i = pick((), at) + (pl.ds(r0, n), slice(None))
                acc[i] = acc[i] + buf[pick((), at, present) + (pl.ds(r0 - start, n), slice(None))]
            walk(full, shifted(xyz, a, rel), body)
        for p in range(3):
            if phase == 0: swap_add(p, 2)
            send(p, 0, 2, 0, 0)
            send(p, 3, 2, 1, 1)
        for p in range(3):
            if phase == 0: swap_add(p, 1)
            send(p, 1, 1, 1, 0)
            if phase == 0: swap_add(p, 3)
            send(p, 4, 3, 0, 1)
        for p in range(3):
            copies[p, 0].wait_recv(); fold(p, 1, 0, 0); send(p, 2, 1, 0, 0)
            copies[p, 3].wait_recv(); fold(p, 3, 1, 1); send(p, 5, 3, 1, 1)
        if phase == 0:
            for p in range(3): swap_add(p, 0)
        for p in range(3):
            copies[p, 1].wait_recv(); fold(p, 0, 1, 0)
            copies[p, 4].wait_recv(); fold(p, 0, 0, 1)
        for p in range(3):
            copies[p, 2].wait_recv(); fold(p, 0, 0, 0)
            copies[p, 5].wait_recv(); fold(p, 0, 1, 1)
    out[...] = acc[pick((), xyz)]
    for c in pend: c.wait_send()

def reduce_scatter(g):
    scratch = [pltpu.VMEM((2, 2, 4, 4, 224, 128), jnp.float32), pltpu.VMEM((2, 2, 4, 4, 224, 128), jnp.float32)]
    for phase in range(3):
        for p in range(3):
            present = ORDERS[p][:3 - phase]
            scratch += [pltpu.VMEM(dims(present) + (PIECES[p][1], 128), jnp.float32)] * 2
    scratch += [pltpu.SemaphoreType.DMA((2,)), pltpu.SemaphoreType.DMA((54,)), pltpu.SemaphoreType.DMA((54,)), pltpu.SemaphoreType.DMA((12,)), pltpu.SemaphoreType.DMA((12,))]
    return pl.pallas_call(
        rs_kernel, out_shape=jax.ShapeDtypeStruct((224, 128), jnp.float32),
        in_specs=[pl.BlockSpec(memory_space=pl.ANY)], out_specs=pl.BlockSpec(memory_space=pltpu.VMEM),
        scratch_shapes=scratch,
        compiler_params=pltpu.CompilerParams(collective_id=1, has_side_effects=True, vmem_limit_bytes=60 << 20),
        name="scatter_grad",
    )(g)


def advance_planes(ext, visc, count, store):
    def body(x, carry):
        mid = [ext[c, x + 1] for c in range(3)]
        nu = visc[x]
        new = []
        for c in range(3):
            up1, lo1 = ext[c, x + 2], ext[c, x]
            up2, lo2 = pltpu.roll(mid[c], 127, 0), pltpu.roll(mid[c], 1, 0)
            up3, lo3 = pltpu.roll(mid[c], 127, 1), pltpu.roll(mid[c], 1, 1)
            laplace = up1 + lo1 + up2 + lo2 + up3 + lo3 - 6.0 * mid[c]
            advect = 0.5 * (mid[0] * (up1 - lo1) + mid[1] * (up2 - lo2) + mid[2] * (up3 - lo3))
            new.append(mid[c] + time_step * (nu * laplace - advect))
        store(x, new)
        return carry
    lax.fori_loop(0, count, body, 0)

def split3(x):
    high = x.astype(jnp.bfloat16); rest = x - high.astype(jnp.float32)
    mid = rest.astype(jnp.bfloat16)
    low = (rest - mid.astype(jnp.float32)).astype(jnp.bfloat16)
    return high, mid, low

def permuted(onehot, x):
    n = x.shape[1]
    parts = jnp.dot(onehot, jnp.concatenate(split3(x), axis=1), preferred_element_type=jnp.float32)
    return parts[:, :n] + parts[:, n:2 * n] + parts[:, 2 * n:]

def swap_groups(x):
    row = lax.broadcasted_iota(jnp.int32, x.shape, 0)
    lane = lax.broadcasted_iota(jnp.int32, x.shape, 1)
    for b in range(4):
        k = 1 << b
        rb, lb = (row >> b) & 1, (lane >> (3 + b)) & 1
        above = pltpu.roll(pltpu.roll(x, 256 - k, 0), 8 * k, 1)
        below = pltpu.roll(pltpu.roll(x, k, 0), 128 - 8 * k, 1)
        x = jnp.where(rb == lb, x, jnp.where(rb == 0, above, below))
    return x

def send_order(assign, sample):
    target = assign // 256
    column = jnp.transpose(jnp.broadcast_to(target, (128, 256)))[:, :1]
    before = lax.broadcasted_iota(jnp.int32, (256, 256), 0) < lax.broadcasted_iota(jnp.int32, (256, 256), 1)
    same = jnp.where((column == target) & before, 1, 0)
    rank = jnp.sum(same, axis=0, keepdims=True)
    dst = lax.broadcasted_iota(jnp.int32, (128, 256), 0)
    rows = [jnp.where((target == dst) & (rank == j), 1.0, 0.0) for j in range(2)]
    chosen = jnp.concatenate(rows, axis=0).astype(jnp.bfloat16)
    patch = jnp.where(sample == lax.broadcasted_iota(jnp.int32, (256, 256), 0), 1.0, 0.0).astype(jnp.bfloat16)
    return lax.dot_general(chosen, patch, (((1,), (1,)), ((), ())), preferred_element_type=jnp.float32).astype(jnp.bfloat16)

def step_kernel(vel, lo, hi, visc, vlo, vhi, assign, sample, nxt, rows, ext, vext, first, order):
    ext[:, 2:10] = vel[...]
    ext[:, 0:2] = lo[...]
    ext[:, 10:12] = hi[...]
    vext[1:9] = visc[...]
    vext[0:1] = vlo[...]
    vext[9:10] = vhi[...]
    order[...] = send_order(assign[...], sample[...])
    def put_first(x, new):
        for c in range(3): first[c, x] = new[c]
    def put_next(x, new):
        for c in range(3): nxt[c, x] = new[c]
    advance_planes(ext, vext, 10, put_first)
    advance_planes(first, visc, 8, put_next)
    def body(i, carry):
        c, p = i // 4, i % 4
        for field, ref, off in ((0, first, 1), (1, nxt, 0)):
            a, b = ref[c, 2 * p + off], ref[c, 2 * p + off + 1]
            pieces = []
            for iy in range(16):
                pieces += [a[iy * 8:iy * 8 + 8], b[iy * 8:iy * 8 + 8]]
            out = permuted(order[...], swap_groups(jnp.concatenate(pieces, axis=0)))
            for j in range(2):
                rows[pl.ds(j * 24 + field * 12 + i, 128, stride=48), :] = out[j * 128:(j + 1) * 128]
        return carry
    lax.fori_loop(0, 12, body, 0)

def steps_and_rows(vel, lo, hi, visc, vlo, vhi, assign, sample):
    f32 = jnp.float32
    return pl.pallas_call(
        step_kernel,
        out_shape=(jax.ShapeDtypeStruct((3, 8, 128, 128), f32), jax.ShapeDtypeStruct((6144, 128), f32)),
        scratch_shapes=[pltpu.VMEM((3, 12, 128, 128), f32), pltpu.VMEM((10, 128, 128), f32), pltpu.VMEM((3, 10, 128, 128), f32), pltpu.VMEM((256, 256), jnp.bfloat16)],
        compiler_params=pltpu.CompilerParams(vmem_limit_bytes=40 << 20),
        name="steps_and_rows",
    )(vel, lo, hi, visc, vlo, vhi, assign, sample)

BLOCK = 232
WIN, WUP, WDN, WOUT = (0, 1536, 4), (6144, 512, 16), (14336, 2048, 4), (22528, 512, 12)
NN = (((1,), (0,)), ((), ())); NT = (((1,), (1,)), ((), ()))

def split2(x):
    high = x.astype(jnp.bfloat16)
    return high, (x - high.astype(jnp.float32)).astype(jnp.bfloat16)

def dot3(a, b, form):
    d = lambda p, q: lax.dot_general(p, q, form, preferred_element_type=jnp.float32)
    return d(a[0], b[0]) + (d(a[0], b[1]) + d(a[1], b[0]))

def put2(refs, value, *at):
    for r, v in zip(refs, split2(value)): r[at] = v

def unpack(flat, spec, hi, lo):
    base, rows, cols = spec
    n = 256
    def body(i, carry):
        for q in range(cols):
            start = base + i * (n * cols) + q
            h, l = split2(flat[pl.ds(start, n, stride=cols), :])
            at = (pl.ds(pl.multiple_of(i * n, n), n), pl.ds(q * 128, 128))
            hi[at] = h; lo[at] = l
        return carry
    lax.fori_loop(0, rows // n, body, 0)

def pack(flat, spec, r0, n, c0, value):
    base, rows, cols = spec
    for q in range(value.shape[1] // 128):
        flat[pl.ds(base + r0 * cols + c0 + q, n, stride=cols), :] = value[:, q * 128:(q + 1) * 128]

def slot_matrix(assign, me):
    mine = (assign // 256) == me
    t = lax.broadcasted_iota(jnp.int32, (128, 256), 1)
    first = jnp.min(jnp.where(mine, t, 512), axis=1, keepdims=True)
    last = jnp.max(jnp.where(mine, t, -1), axis=1, keepdims=True)
    slot = assign % 256
    cols = [jnp.sum(jnp.where(t == at, slot, 0), axis=1, keepdims=True) for at in (first, last)]
    want = jnp.concatenate([jnp.where(c == t, 1.0, 0.0) for c in cols], axis=0)
    return jnp.transpose(want).astype(jnp.bfloat16)

def learn_kernel(got, gathered, pred, grads, flat, asg, win, winl, wup, wupl, wdn, wdnl, wout, woutl,
                 x, tgt, xs, xsl, hid, pre, a5, a5l, state, state2, rowsc, sem, osem):
    me = lax.axis_index("group") * 32 + lax.axis_index("dev")
    ac = pltpu.make_async_copy(gathered.at[:, pl.ds(224, 8), :], asg, sem.at[0])
    wc = pltpu.make_async_copy(gathered.at[:, pl.ds(0, 224), :], flat.reshape(128, 224, 128), sem.at[1])
    ac.start(); wc.start()
    ac.wait()
    assign = jnp.concatenate([asg[:, 0, :], asg[:, 1, :]], axis=1).astype(jnp.int32)
    place = slot_matrix(assign, me)
    rowsc[...] = place
    for field, ref in ((0, x), (1, tgt)):
        for k in range(12):
            src = jnp.concatenate([got[pl.ds(j * 24 + field * 12 + k, 128, stride=48), :] for j in range(2)], axis=0)
            ref[:, k * 128:(k + 1) * 128] = permuted(rowsc[...], src)
    wc.wait()
    unpack(flat, WIN, win, winl)
    unpack(flat, WUP, wup, wupl)
    unpack(flat, WDN, wdn, wdnl)
    unpack(flat, WOUT, wout, woutl)
    put2((xs, xsl), x[...], slice(None), slice(None))
    for n in range(2):
        at = (slice(None), pl.ds(n * 256, 256))
        state[at] = dot3((xs[...], xsl[...]), (win[at], winl[at]), NN)
    s = state[...]
    r = lax.rsqrt(jnp.mean(s * s, axis=1, keepdims=True) + norm_epsilon)
    put2((a5, a5l), s * r, slice(None), slice(None))
    c1, c2 = 0.7978845608028654, 0.044715
    def up(n, carry):
        at = (slice(None), pl.ds(pl.multiple_of(n * 256, 256), 256))
        p = dot3((a5[...], a5l[...]), (wup[at], wupl[at]), NN)
        pre[at] = p
        hid[at] = 0.5 * p * (1.0 + jnp.tanh(c1 * (p + c2 * (p * p * p))))
        return carry
    lax.fori_loop(0, 8, up, 0)
    def down(n, acc):
        at = (slice(None), pl.ds(pl.multiple_of(n * 256, 256), 256))
        wat = (pl.ds(pl.multiple_of(n * 256, 256), 256), slice(None))
        return acc + dot3(split2(hid[at]), (wdn[wat], wdnl[wat]), NN)
    state2[...] = lax.fori_loop(0, 8, down, s)
    s2 = split2(state2[...])
    def outp(n, carry):
        at = (slice(None), pl.ds(pl.multiple_of(n * 256, 256), 256))
        g = x[at] + dot3(s2, (wout[at], woutl[at]), NN)
        pred[at] = g
        tgt[at] = (g - tgt[at]) * (1.0 / 256.0)
        return carry
    lax.fori_loop(0, 6, outp, 0)
    s2t = split2(jnp.transpose(state2[...]))
    def gout(n, acc):
        at = (slice(None), pl.ds(pl.multiple_of(n * 256, 256), 256))
        e = split2(tgt[at])
        pack(flat, WOUT, 0, 512, n * 2, dot3(s2t, e, NN))
        return acc + dot3(e, (wout[at], woutl[at]), NT)
    ds2 = lax.fori_loop(0, 6, gout, jnp.zeros((256, 512), jnp.float32))
    state2[...] = ds2
    put2((xs, xsl), ds2, slice(None), pl.ds(0, 512))
    dss = lambda: (xs[:, :512], xsl[:, :512])
    normt = jnp.transpose(state[...] * r)
    nt = split2(normt)
    def hidden(n, acc):
        at = (slice(None), pl.ds(pl.multiple_of(n * 256, 256), 256))
        wat = (pl.ds(pl.multiple_of(n * 256, 256), 256), slice(None))
        d = dss()
        pack(flat, WDN, n * 256, 256, 0, dot3(split2(jnp.transpose(hid[at])), d, NN))
        dh = dot3(d, (wdn[wat], wdnl[wat]), NT)
        p = pre[at]
        th = jnp.tanh(c1 * (p + c2 * (p * p * p)))
        dp = dh * (0.5 * (1.0 + th) + 0.5 * p * (1.0 - th * th) * (c1 * (1.0 + (3.0 * c2) * (p * p))))
        dps = split2(dp)
        pack(flat, WUP, 0, 512, n * 2, dot3(nt, dps, NN))
        return acc + dot3(dps, (wup[at], wupl[at]), NT)
    dn = lax.fori_loop(0, 8, hidden, jnp.zeros((256, 512), jnp.float32))
    norm = state[...] * r
    ds = state2[...] + r * (dn - norm * jnp.mean(dn * norm, axis=1, keepdims=True))
    put2((a5, a5l), ds, slice(None), slice(None))
    def gin(n, carry):
        at = (slice(None), pl.ds(pl.multiple_of(n * 256, 256), 256))
        pack(flat, WIN, n * 256, 256, 0, dot3(split2(jnp.transpose(x[at])), (a5[...], a5l[...]), NN))
        return carry
    lax.fori_loop(0, 6, gin, 0)
    oc = pltpu.make_async_copy(flat, grads, osem)
    oc.start(); oc.wait()

def learn(got, gathered):
    f32, b16 = jnp.float32, jnp.bfloat16
    V = pltpu.VMEM
    both = lambda *s: [V(s, b16), V(s, b16)]
    return pl.pallas_call(
        learn_kernel,
        out_shape=(jax.ShapeDtypeStruct((256, 1536), f32), jax.ShapeDtypeStruct((28672, 128), f32)),
        in_specs=[pl.BlockSpec(memory_space=pltpu.VMEM), pl.BlockSpec(memory_space=pl.ANY)],
        out_specs=(pl.BlockSpec(memory_space=pltpu.VMEM), pl.BlockSpec(memory_space=pl.ANY)),
        scratch_shapes=[V((28672, 128), f32), V((128, 8, 128), f32)] + both(1536, 512) + both(512, 2048) + both(2048, 512) + both(512, 1536)
            + [V((256, 1536), f32), V((256, 1536), f32)] + both(256, 1536) + [V((256, 2048), f32), V((256, 2048), f32)] + both(256, 512)
            + [V((256, 512), f32), V((256, 512), f32), V((256, 256), b16), pltpu.SemaphoreType.DMA((2,)), pltpu.SemaphoreType.DMA],
        compiler_params=pltpu.CompilerParams(vmem_limit_bytes=60 << 20),
        name="learn",
    )(got, gathered)

def adam(shard, grad, moment, second):
    new_m = beta_first * moment + (1.0 - beta_first) * grad
    new_v = beta_second * second + (1.0 - beta_second) * grad * grad
    update = (
        new_m
        / (1.0 - beta_first**adam_count)
        / (jnp.sqrt(new_v / (1.0 - beta_second**adam_count)) + adam_epsilon)
    )
    return (shard - learn_rate * update, new_m, new_v)

def edges(value, width, dim):
    both = ("group", "dev")
    size, length = lax.axis_size(both), value.shape[dim]
    up = [(i, i + 1) for i in range(size - 1)]
    last = lax.slice_in_dim(value, length - width, length, axis=dim)
    initial = lax.slice_in_dim(value, 0, width, axis=dim)
    return lax.ppermute(last, both, up), lax.ppermute(initial, both, [(b, a) for a, b in up])

def local(velocity, viscosity, sample_idx, assign, params, adam_m, adam_v):
    lo, hi = edges(velocity, 2, 1)
    vlo, vhi = edges(viscosity, 1, 0)
    velocity_next, rows = steps_and_rows(velocity, lo, hi, viscosity, vlo, vhi, assign, sample_idx)
    slots = jnp.pad(assign.reshape(2, 128).astype(jnp.float32), ((0, 6), (0, 0)))
    shard = jnp.concatenate([params.reshape(224, 128), slots], axis=0)
    shard, rows = lax.optimization_barrier((shard, rows))
    got = lax.all_to_all(rows.reshape(128, 48, 128), ("group", "dev"), 0, 0, tiled=True)
    gathered = all_gather(shard).reshape(128, 232, 128)
    prediction, grad = learn(got.reshape(6144, 128), gathered)
    mine = reduce_scatter(grad.reshape(2, 2, 2, 4, 4, 224, 128)).reshape(-1)
    new_params, new_m, new_v = adam(params, mine, adam_m, adam_v)
    return (velocity_next, prediction, new_params, new_m, new_v)


def solution(mesh):
    placed = (
        P(None, ("group", "dev"), None, None),
        P(("group", "dev"), None, None),
        P(("group", "dev"), None),
        P(("group", "dev"), None),
        P(("group", "dev")),
        P(("group", "dev")),
        P(("group", "dev")),
    )
    return jax.shard_map(
        local,
        mesh=mesh,
        in_specs=placed,
        out_specs=(
            P(None, ("group", "dev"), None, None),
            P(("group", "dev"), None),
            P(("group", "dev")),
            P(("group", "dev")),
            P(("group", "dev")),
        ),
        check_vma=False,
    )
```

```python
import jax
import jax.numpy as jnp
from jax import lax
from jax.experimental import pallas as pl
from jax.experimental.pallas import tpu as pltpu
from jax.sharding import PartitionSpec as P

time_step = 0.5
norm_epsilon = 1e-06
beta_first = 0.9
beta_second = 0.95
learn_rate = 0.01
adam_epsilon = 1e-08
adam_count = 10

MESH = pl.DeviceIdType.MESH
PIECES = ((0, 72), (72, 80), (152, 72))
ORDERS = ((0, 1, 2), (1, 2, 0), (2, 0, 1))

def coords():
    g = lax.axis_index("group"); d = lax.axis_index("dev")
    return (d % 4, (d // 4) % 4, (g // 2) * 2 + d // 16), g % 2

def ident(xyz, core):
    x, y, z = xyz
    return ((z // 2) * 2 + core, (z % 2) * 16 + y * 4 + x)

def shifted(xyz, axis, by):
    out = list(xyz); out[axis] = (xyz[axis] + by) % 4
    return tuple(out)

def neighbours(xyz, core):
    ids = [ident(shifted(xyz, a, s), core) for a in range(3) for s in (1, 3)]
    return ids + [ident(xyz, 1 - core)]

def enter(xyz, core):
    barrier = pltpu.get_barrier_semaphore()
    ids = neighbours(xyz, core)
    for i in ids:
        pl.semaphore_signal(barrier, inc=1, device_id=i, device_id_type=MESH)
    pl.semaphore_wait(barrier, len(ids))

def region(ref, full, xyz, core, r0, n):
    x = slice(None) if 0 in full else xyz[0]
    y = slice(None) if 1 in full else xyz[1]
    zh = slice(None) if 2 in full else xyz[2] // 2
    zl = slice(None) if 2 in full else xyz[2] % 2
    return ref.at[zh, core, zl, y, x, pl.ds(r0, n), :]

def halves(piece, pieces=PIECES):
    r0, n = pieces[piece]
    n0 = (n // 16) * 8 if n % 16 else n // 2
    return (r0, n0), (r0 + n0, n - n0)


def pick(full, xyz, present=(0, 1, 2)):
    out = []
    if 2 in present: out += [slice(None)] * 2 if 2 in full else [xyz[2] // 2, xyz[2] % 2]
    if 1 in present: out += [slice(None)] if 1 in full else [xyz[1]]
    if 0 in present: out += [slice(None)] if 0 in full else [xyz[0]]
    return tuple(out)

def walk(full, xyz, body):
    full = tuple(full)
    if not full:
        body(xyz); return
    def step(i, carry):
        at = list(xyz)
        for k, a in enumerate(full):
            at[a] = (i // (4 ** k)) % 4
        body(tuple(at)); return carry
    lax.fori_loop(0, 4 ** len(full), step, 0)

def dims(present):
    out = ()
    if 2 in present: out += (2, 2)
    if 1 in present: out += (4,)
    if 0 in present: out += (4,)
    return out

def rs_kernel(g, out, acc, crecv, *rest):
    bufs = {}; k = 0
    for phase in range(3):
        for p in range(3):
            for side in range(2):
                bufs[phase, p, side] = rest[k]; k += 1
    lsem, ssem, rsem, cs, cr = rest[k:]
    xyz, core = coords()
    load = [pltpu.make_async_copy(g.at[zh, core], acc.at[zh], lsem.at[zh]) for zh in range(2)]
    for c in load: c.start()
    enter(xyz, core)
    sib = ident(xyz, 1 - core)
    swaps = {}; pend = []
    for rel in (2, 1, 3, 0):
        for p in range(3):
            a = ORDERS[p][2]; full = ORDERS[p][:2]; r0, n = PIECES[p]
            at = shifted(xyz, a, rel); slot = len(swaps)
            i = pick(full, at)
            c = pltpu.make_async_remote_copy(src_ref=g.at[(i[0], 1 - core) + i[1:] + (pl.ds(r0, n),)], dst_ref=crecv.at[i + (pl.ds(r0, n),)],
                send_sem=cs.at[slot], recv_sem=cr.at[slot], device_id=sib, device_id_type=MESH)
            c.start(); swaps[p, rel] = c; pend.append(c)
    for c in load: c.wait()

    def swap_add(p, rel):
        a = ORDERS[p][2]; r0, n = PIECES[p]
        swaps[p, rel].wait_recv()
        def body(at):
            i = pick((), at) + (pl.ds(r0, n), slice(None))
            acc[i] = acc[i] + crecv[i]
        walk(ORDERS[p][:2], shifted(xyz, a, rel), body)

    for phase in range(3):
        def parts(p):
            a = ORDERS[p][2 - phase]; full = ORDERS[p][:2 - phase]; present = full + (a,)
            R = ident(shifted(xyz, a, 1), core); L = ident(shifted(xyz, a, 3), core)
            return a, full, present, R, L, halves(p), ((phase * 3 + p) * 6), PIECES[p][0]
        copies = {}
        def send(p, kind, rel, half, side):
            a, full, present, R, L, hs, base, start = parts(p)
            at = shifted(xyz, a, rel); r0, n = hs[half]
            c = pltpu.make_async_remote_copy(src_ref=acc.at[pick(full, at) + (pl.ds(r0, n),)],
                dst_ref=bufs[phase, p, side].at[pick(full, at, present) + (pl.ds(r0 - start, n),)],
                send_sem=ssem.at[base + kind], recv_sem=rsem.at[base + kind],
                device_id=(R, L)[side], device_id_type=MESH)
            c.start(); copies[p, kind] = c; pend.append(c)
        def fold(p, rel, half, side):
            a, full, present, R, L, hs, base, start = parts(p)
            buf = bufs[phase, p, side]; r0, n = hs[half]
            def body(at):
                i = pick((), at) + (pl.ds(r0, n), slice(None))
                acc[i] = acc[i] + buf[pick((), at, present) + (pl.ds(r0 - start, n), slice(None))]
            walk(full, shifted(xyz, a, rel), body)
        for p in range(3):
            if phase == 0: swap_add(p, 2)
            send(p, 0, 2, 0, 0)
            send(p, 3, 2, 1, 1)
        for p in range(3):
            if phase == 0: swap_add(p, 1)
            send(p, 1, 1, 1, 0)
            if phase == 0: swap_add(p, 3)
            send(p, 4, 3, 0, 1)
        for p in range(3):
            copies[p, 0].wait_recv(); fold(p, 1, 0, 0); send(p, 2, 1, 0, 0)
            copies[p, 3].wait_recv(); fold(p, 3, 1, 1); send(p, 5, 3, 1, 1)
        if phase == 0:
            for p in range(3): swap_add(p, 0)
        for p in range(3):
            copies[p, 1].wait_recv(); fold(p, 0, 1, 0)
            copies[p, 4].wait_recv(); fold(p, 0, 0, 1)
        for p in range(3):
            copies[p, 2].wait_recv(); fold(p, 0, 0, 0)
            copies[p, 5].wait_recv(); fold(p, 0, 1, 1)
    out[...] = acc[pick((), xyz)]
    for c in pend: c.wait_send()

def reduce_scatter(g):
    scratch = [pltpu.VMEM((2, 2, 4, 4, 224, 128), jnp.float32), pltpu.VMEM((2, 2, 4, 4, 224, 128), jnp.float32)]
    for phase in range(3):
        for p in range(3):
            present = ORDERS[p][:3 - phase]
            scratch += [pltpu.VMEM(dims(present) + (PIECES[p][1], 128), jnp.float32)] * 2
    scratch += [pltpu.SemaphoreType.DMA((2,)), pltpu.SemaphoreType.DMA((54,)), pltpu.SemaphoreType.DMA((54,)), pltpu.SemaphoreType.DMA((12,)), pltpu.SemaphoreType.DMA((12,))]
    return pl.pallas_call(
        rs_kernel, out_shape=jax.ShapeDtypeStruct((224, 128), jnp.float32),
        in_specs=[pl.BlockSpec(memory_space=pl.ANY)], out_specs=pl.BlockSpec(memory_space=pltpu.VMEM),
        scratch_shapes=scratch,
        compiler_params=pltpu.CompilerParams(collective_id=1, has_side_effects=True, vmem_limit_bytes=60 << 20),
        name="scatter_grad",
    )(g)


def advance_planes(ext, visc, count, store):
    def body(x, carry):
        mid = [ext[c, x + 1] for c in range(3)]
        nu = visc[x]
        new = []
        for c in range(3):
            up1, lo1 = ext[c, x + 2], ext[c, x]
            up2, lo2 = pltpu.roll(mid[c], 127, 0), pltpu.roll(mid[c], 1, 0)
            up3, lo3 = pltpu.roll(mid[c], 127, 1), pltpu.roll(mid[c], 1, 1)
            laplace = up1 + lo1 + up2 + lo2 + up3 + lo3 - 6.0 * mid[c]
            advect = 0.5 * (mid[0] * (up1 - lo1) + mid[1] * (up2 - lo2) + mid[2] * (up3 - lo3))
            new.append(mid[c] + time_step * (nu * laplace - advect))
        store(x, new)
        return carry
    lax.fori_loop(0, count, body, 0)

def split3(x):
    high = x.astype(jnp.bfloat16); rest = x - high.astype(jnp.float32)
    mid = rest.astype(jnp.bfloat16)
    low = (rest - mid.astype(jnp.float32)).astype(jnp.bfloat16)
    return high, mid, low

def permuted(onehot, x):
    n = x.shape[1]
    parts = jnp.dot(onehot, jnp.concatenate(split3(x), axis=1), preferred_element_type=jnp.float32)
    return parts[:, :n] + parts[:, n:2 * n] + parts[:, 2 * n:]

def swap_groups(x):
    row = lax.broadcasted_iota(jnp.int32, x.shape, 0)
    lane = lax.broadcasted_iota(jnp.int32, x.shape, 1)
    for b in range(4):
        k = 1 << b
        rb, lb = (row >> b) & 1, (lane >> (3 + b)) & 1
        above = pltpu.roll(pltpu.roll(x, 256 - k, 0), 8 * k, 1)
        below = pltpu.roll(pltpu.roll(x, k, 0), 128 - 8 * k, 1)
        x = jnp.where(rb == lb, x, jnp.where(rb == 0, above, below))
    return x

def send_order(assign, sample):
    target = assign // 256
    column = jnp.transpose(jnp.broadcast_to(target, (128, 256)))[:, :1]
    before = lax.broadcasted_iota(jnp.int32, (256, 256), 0) < lax.broadcasted_iota(jnp.int32, (256, 256), 1)
    same = jnp.where((column == target) & before, 1, 0)
    rank = jnp.sum(same, axis=0, keepdims=True)
    dst = lax.broadcasted_iota(jnp.int32, (128, 256), 0)
    rows = [jnp.where((target == dst) & (rank == j), 1.0, 0.0) for j in range(2)]
    chosen = jnp.concatenate(rows, axis=0).astype(jnp.bfloat16)
    patch = jnp.where(sample == lax.broadcasted_iota(jnp.int32, (256, 256), 0), 1.0, 0.0).astype(jnp.bfloat16)
    return lax.dot_general(chosen, patch, (((1,), (1,)), ((), ())), preferred_element_type=jnp.float32).astype(jnp.bfloat16)

GATHER = ((0, 72), (72, 80), (152, 80))

def front_kernel(shard, vel, visc, assign, sample, nxt, out, got, ext, vext, first, order, s0, *rest):
    s1, s2, s3, relay = rest[0:3], rest[3:6], rest[6:9], rest[9:27]
    hs, hr, lsem, ssem, rsem, cs, cr, xs, xr, xl = rest[27:]
    xyz, core = coords()
    me = lax.axis_index("group") * 32 + lax.axis_index("dev")
    after, before = (me + 1) % 128, (me + 127) % 128
    after_id, before_id = (after // 32, after % 32), (before // 32, before % 32)
    own = pltpu.make_async_copy(shard, out.at[xyz[2] // 2, core, xyz[2] % 2, xyz[1], xyz[0]], lsem)
    own.start()
    barrier = pltpu.get_barrier_semaphore()
    ids = neighbours(xyz, core) + [after_id, before_id]
    for i in ids:
        pl.semaphore_signal(barrier, inc=1, device_id=i, device_id_type=MESH)
    ext[:, 2:10] = vel[...]
    vext[1:9] = visc[...]
    pl.semaphore_wait(barrier, len(ids))
    sib = ident(xyz, 1 - core)
    pend = []

    def remote(src, dst, s, r, to):
        c = pltpu.make_async_remote_copy(src_ref=src, dst_ref=dst, send_sem=s, recv_sem=r, device_id=to, device_id_type=MESH)
        c.start(); pend.append(c)
        return c

    halo = [remote(vel.at[:, 6:8], ext.at[:, 0:2], hs.at[0], hr.at[0], after_id),
            remote(vel.at[:, 0:2], ext.at[:, 10:12], hs.at[1], hr.at[1], before_id),
            remote(visc.at[7:8], vext.at[0:1], hs.at[2], hr.at[2], after_id),
            remote(visc.at[0:1], vext.at[9:10], hs.at[3], hr.at[3], before_id)]

    sibs = []
    def to_sib(src):
        k = len(sibs)
        sibs.append(remote(src, src, cs.at[k], cr.at[k], sib))
    steps = {}
    def around(p, phase):
        a = ORDERS[p][phase]; full = ORDERS[p][:phase]
        at = [shifted(xyz, a, k) for k in range(4)]
        return full, at, ident(at[1], core), ident(at[3], core), halves(p, GATHER), (phase * 3 + p) * 6, GATHER[p]
    def g_send(p, phase, kind, at, half, to):
        full, _, _, _, hs_, base, _ = around(p, phase)
        r0, n = hs_[half]
        src = region(out, full, at, core, r0, n)
        steps[p, phase, kind] = remote(src, src, ssem.at[base + kind], rsem.at[base + kind], to)
    def g_start(phase):
        for p in range(3):
            full, at, R, L, hv, base, (r0, n) = around(p, phase)
            g_send(p, phase, 0, at[0], 0, R)
            g_send(p, phase, 3, at[0], 1, L)
            g_send(p, phase, 1, at[0], 1, R)
            g_send(p, phase, 4, at[0], 0, L)
            if phase == 2: to_sib(region(out, full, at[0], core, r0, n))
    def g_forward(phase):
        for p in range(3):
            full, at, R, L, hv, base, _ = around(p, phase)
            steps[p, phase, 0].wait_recv(); g_send(p, phase, 2, at[3], 0, R)
            steps[p, phase, 3].wait_recv(); g_send(p, phase, 5, at[1], 1, L)
    def g_near(phase):
        for p in range(3):
            full, at, R, L, hv, base, (r0, n) = around(p, phase)
            steps[p, phase, 1].wait_recv(); steps[p, phase, 4].wait_recv()
            if phase == 2:
                to_sib(region(out, full, at[3], core, r0, n))
                to_sib(region(out, full, at[1], core, r0, n))
    def g_far(phase):
        for p in range(3):
            full, at, R, L, hv, base, (r0, n) = around(p, phase)
            steps[p, phase, 2].wait_recv(); steps[p, phase, 5].wait_recv()
            if phase == 2: to_sib(region(out, full, at[2], core, r0, n))

    moves, selfs = {}, {}
    def x_core():
        blocks = s0.reshape(2, 2, 2, 4, 4, 48, 128)
        for p in range(3):
            for zh in range(2):
                k = p * 2 + zh
                rows = pl.ds(16 * p, 16)
                moves[p, 0, zh] = remote(blocks.at[zh, 1 - core, :, :, :, rows], s1[p].at[core, zh], xs.at[k], xr.at[k], sib)
                selfs[p, 0, zh] = pltpu.make_async_copy(blocks.at[zh, core, :, :, :, rows], s1[p].at[core, zh], xl.at[k])
                selfs[p, 0, zh].start()
    def stage(p, s):
        a = ORDERS[p][s - 1]; others = ORDERS[p][s:]
        src = (s1, s2, s3)[s - 1][p]
        dst = got.at[p] if s == 3 else (s2, s3)[s - 1][p]
        at = [shifted(xyz, a, k) for k in range(4)]
        left = (slice(None),) * s
        def part(k, r0, n): return src.at[left + pick(others, at[k], (a,) + others) + (pl.ds(r0, n),)]
        free = (slice(None),) * (s + len(dims(others)))
        def land(k, r0, n): return dst.at[(at[k][a],) + free + (pl.ds(r0, n),)]
        return part, land, ident(at[1], core), ident(at[3], core), 6 + ((s - 1) * 3 + p) * 6
    def x_start(s):
        for p in range(3):
            part, land, R, L, base = stage(p, s)
            if s == 1:
                for zh in range(2): moves[p, 0, zh].wait_recv(); selfs[p, 0, zh].wait()
            else:
                for k in (0, 1, 4, 5): moves[p, s - 1, k].wait_recv()
                selfs[p, s - 1].wait()
            def mv(k, src, dst, to): moves[p, s, k] = remote(src, dst, xs.at[base + k], xr.at[base + k], to)
            via = relay[((s - 1) * 3 + p) * 2], relay[((s - 1) * 3 + p) * 2 + 1]
            mv(2, part(2, 0, 8), via[0], R)
            mv(3, part(2, 8, 8), via[1], L)
            mv(0, part(1, 0, 16), land(0, 0, 16), R)
            mv(1, part(3, 0, 16), land(0, 0, 16), L)
            c = pltpu.make_async_copy(part(0, 0, 16), land(0, 0, 16), xl.at[6 + (s - 1) * 3 + p])
            c.start(); selfs[p, s] = c
    def x_relay(s):
        for p in range(3):
            part, land, R, L, base = stage(p, s)
            via = relay[((s - 1) * 3 + p) * 2], relay[((s - 1) * 3 + p) * 2 + 1]
            moves[p, s, 2].wait_recv()
            moves[p, s, 4] = remote(via[0], land(3, 0, 8), xs.at[base + 4], xr.at[base + 4], R)
            moves[p, s, 3].wait_recv()
            moves[p, s, 5] = remote(via[1], land(1, 8, 8), xs.at[base + 5], xr.at[base + 5], L)
    def x_finish():
        for p in range(3):
            for k in (0, 1, 4, 5): moves[p, 3, k].wait_recv()
            selfs[p, 3].wait()

    own.wait()
    g_start(0)
    order[...] = send_order(assign[...], sample[...])
    for c in halo: c.wait_recv()
    lower = jnp.where(me > 0, 1.0, 0.0); upper = jnp.where(me < 127, 1.0, 0.0)
    ext[:, 0:2] = ext[:, 0:2] * lower
    vext[0:1] = vext[0:1] * lower
    ext[:, 10:12] = ext[:, 10:12] * upper
    vext[9:10] = vext[9:10] * upper
    g_forward(0)
    def put_first(x, new):
        for c in range(3): first[c, x] = new[c]
    def put_next(x, new):
        for c in range(3): nxt[c, x] = new[c]
    advance_planes(ext, vext, 10, put_first)
    g_near(0); g_far(0)
    g_start(1)
    advance_planes(first, visc, 8, put_next)
    g_forward(1)
    def body(i, carry):
        c, q = i // 4, i % 4
        for field, ref, off in ((0, first, 1), (1, nxt, 0)):
            a, b = ref[c, 2 * q + off], ref[c, 2 * q + off + 1]
            pieces = []
            for iy in range(16):
                pieces += [a[iy * 8:iy * 8 + 8], b[iy * 8:iy * 8 + 8]]
            res = permuted(order[...], swap_groups(jnp.concatenate(pieces, axis=0)))
            for j in range(2):
                s0[pl.ds(j * 24 + field * 12 + i, 128, stride=48), :] = res[j * 128:(j + 1) * 128]
        return carry
    lax.fori_loop(0, 6, body, 0)
    g_near(1); g_far(1)
    g_start(2)
    lax.fori_loop(6, 12, body, 0)
    x_core()
    g_forward(2)
    x_start(1)
    g_near(2)
    x_relay(1)
    x_start(2)
    g_far(2)
    x_relay(2)
    x_start(3)
    x_relay(3)
    x_finish()
    for c in sibs: c.wait_recv()
    for c in pend: c.wait_send()

def front(shard, vel, visc, assign, sample):
    f32, V = jnp.float32, pltpu.VMEM
    scratch = [V((3, 12, 128, 128), f32), V((10, 128, 128), f32), V((3, 10, 128, 128), f32), V((256, 256), jnp.bfloat16), V((6144, 128), f32)]
    scratch += [V((2, 2, 2, 4, 4, 16, 128), f32)] * 3
    for s in (2, 3):
        for p in range(3):
            scratch.append(V((4,) * (s - 1) + (2,) + dims(ORDERS[p][s - 1:]) + (16, 128), f32))
    for s in (1, 2, 3):
        for p in range(3):
            scratch += [V((4,) * (s - 1) + (2,) + dims(ORDERS[p][s:]) + (8, 128), f32)] * 2
    D = pltpu.SemaphoreType.DMA
    scratch += [D((4,)), D((4,)), D, D((54,)), D((54,)), D((12,)), D((12,)), D((60,)), D((60,)), D((15,))]
    A = pl.BlockSpec(memory_space=pl.ANY); M = pl.BlockSpec(memory_space=pltpu.VMEM)
    return pl.pallas_call(
        front_kernel,
        out_shape=(jax.ShapeDtypeStruct((3, 8, 128, 128), f32), jax.ShapeDtypeStruct((2, 2, 2, 4, 4, 232, 128), f32),
                   jax.ShapeDtypeStruct((3, 4, 4, 4, 2, 16, 128), f32)),
        in_specs=[A, M, M, M, M], out_specs=(M, A, A), scratch_shapes=scratch,
        compiler_params=pltpu.CompilerParams(collective_id=0, has_side_effects=True, vmem_limit_bytes=58 << 20),
        name="front",
    )(shard, vel, visc, assign, sample)

BLOCK = 232
WIN, WUP, WDN, WOUT = (0, 1536, 4), (6144, 512, 16), (14336, 2048, 4), (22528, 512, 12)
NN = (((1,), (0,)), ((), ())); NT = (((1,), (1,)), ((), ()))

def split2(x):
    high = x.astype(jnp.bfloat16)
    return high, (x - high.astype(jnp.float32)).astype(jnp.bfloat16)

def dot3(a, b, form):
    d = lambda p, q: lax.dot_general(p, q, form, preferred_element_type=jnp.float32)
    return d(a[0], b[0]) + (d(a[0], b[1]) + d(a[1], b[0]))

def put2(refs, value, *at):
    for r, v in zip(refs, split2(value)): r[at] = v

def unpack(flat, spec, hi, lo):
    base, rows, cols = spec
    n = 256
    def body(i, carry):
        for q in range(cols):
            start = base + i * (n * cols) + q
            h, l = split2(flat[pl.ds(start, n, stride=cols), :])
            at = (pl.ds(pl.multiple_of(i * n, n), n), pl.ds(q * 128, 128))
            hi[at] = h; lo[at] = l
        return carry
    lax.fori_loop(0, rows // n, body, 0)

def pack(flat, spec, r0, n, c0, value):
    base, rows, cols = spec
    for q in range(value.shape[1] // 128):
        flat[pl.ds(base + r0 * cols + c0 + q, n, stride=cols), :] = value[:, q * 128:(q + 1) * 128]

def slot_matrices(assign, me):
    mine = (assign // 256) == me
    t = lax.broadcasted_iota(jnp.int32, (128, 256), 1)
    first = jnp.min(jnp.where(mine, t, 512), axis=1, keepdims=True)
    last = jnp.max(jnp.where(mine, t, -1), axis=1, keepdims=True)
    slot = assign % 256
    cols = [jnp.sum(jnp.where(t == at, slot, 0), axis=1, keepdims=True) for at in (first, last)]
    want = [jnp.where(c == t, 1.0, 0.0).astype(jnp.bfloat16) for c in cols]
    k = lax.broadcasted_iota(jnp.int32, (128, 128), 0)
    src = lax.broadcasted_iota(jnp.int32, (128, 128), 1)
    moved = []
    for p in range(3):
        co = {ORDERS[p][2]: k // 32, ORDERS[p][1]: (k // 8) % 4, ORDERS[p][0]: (k // 2) % 4}
        flat = (co[2] // 2) * 64 + (k % 2) * 32 + (co[2] % 2) * 16 + co[1] * 4 + co[0]
        perm = jnp.where(flat == src, 1.0, 0.0).astype(jnp.bfloat16)
        moved.append([jnp.dot(perm, w, preferred_element_type=jnp.float32) for w in want])
    return [jnp.transpose(jnp.concatenate([moved[p0][0], moved[p1][1]], axis=0)).astype(jnp.bfloat16) for p0, p1 in PAIRS]

PAIRS = ((0, 1), (0, 2), (1, 2))

def learn_kernel(got, gathered, pred, grads, flat, asg, win, winl, wup, wupl, wdn, wdnl, wout, woutl,
                 x, tgt, xs, xsl, hid, pre, a5, a5l, state, state2, rowsc, sem, osem):
    me = lax.axis_index("group") * 32 + lax.axis_index("dev")
    ac = pltpu.make_async_copy(gathered.at[:, pl.ds(224, 8), :], asg, sem.at[0])
    wc = pltpu.make_async_copy(gathered.at[:, pl.ds(0, 224), :], flat.reshape(128, 224, 128), sem.at[1])
    ac.start(); wc.start()
    ac.wait()
    assign = jnp.concatenate([asg[:, 0, :], asg[:, 1, :]], axis=1).astype(jnp.int32)
    for i, place in enumerate(slot_matrices(assign, me)): rowsc[i] = place
    for field, ref in ((0, x), (1, tgt)):
        for k in range(12):
            col = [j * 24 + field * 12 + k for j in range(2)]
            src = jnp.concatenate([got[pl.ds((c // 16) * 2048 + c % 16, 128, stride=16), :] for c in col], axis=0)
            ref[:, k * 128:(k + 1) * 128] = permuted(rowsc[(col[0]) // 8], src)
    wc.wait()
    unpack(flat, WIN, win, winl)
    unpack(flat, WUP, wup, wupl)
    unpack(flat, WDN, wdn, wdnl)
    unpack(flat, WOUT, wout, woutl)
    put2((xs, xsl), x[...], slice(None), slice(None))
    for n in range(2):
        at = (slice(None), pl.ds(n * 256, 256))
        state[at] = dot3((xs[...], xsl[...]), (win[at], winl[at]), NN)
    s = state[...]
    r = lax.rsqrt(jnp.mean(s * s, axis=1, keepdims=True) + norm_epsilon)
    put2((a5, a5l), s * r, slice(None), slice(None))
    c1, c2 = 0.7978845608028654, 0.044715
    def up(n, carry):
        at = (slice(None), pl.ds(pl.multiple_of(n * 256, 256), 256))
        p = dot3((a5[...], a5l[...]), (wup[at], wupl[at]), NN)
        pre[at] = p
        hid[at] = 0.5 * p * (1.0 + jnp.tanh(c1 * (p + c2 * (p * p * p))))
        return carry
    lax.fori_loop(0, 8, up, 0)
    def down(n, acc):
        at = (slice(None), pl.ds(pl.multiple_of(n * 256, 256), 256))
        wat = (pl.ds(pl.multiple_of(n * 256, 256), 256), slice(None))
        return acc + dot3(split2(hid[at]), (wdn[wat], wdnl[wat]), NN)
    state2[...] = lax.fori_loop(0, 8, down, s)
    s2 = split2(state2[...])
    def outp(n, carry):
        at = (slice(None), pl.ds(pl.multiple_of(n * 256, 256), 256))
        g = x[at] + dot3(s2, (wout[at], woutl[at]), NN)
        pred[at] = g
        tgt[at] = (g - tgt[at]) * (1.0 / 256.0)
        return carry
    lax.fori_loop(0, 6, outp, 0)
    ships = []
    def ship(k, spec):
        rows = pl.ds(spec[0], spec[1] * spec[2])
        ships.append(pltpu.make_async_copy(flat.at[rows], grads.at[rows], osem.at[k])); ships[-1].start()
    s2t = split2(jnp.transpose(state2[...]))
    def gout(n, acc):
        at = (slice(None), pl.ds(pl.multiple_of(n * 256, 256), 256))
        e = split2(tgt[at])
        pack(flat, WOUT, 0, 512, n * 2, dot3(s2t, e, NN))
        return acc + dot3(e, (wout[at], woutl[at]), NT)
    ds2 = lax.fori_loop(0, 6, gout, jnp.zeros((256, 512), jnp.float32))
    ship(0, WOUT)
    state2[...] = ds2
    put2((xs, xsl), ds2, slice(None), pl.ds(0, 512))
    dss = lambda: (xs[:, :512], xsl[:, :512])
    normt = jnp.transpose(state[...] * r)
    nt = split2(normt)
    def hidden(n, acc):
        at = (slice(None), pl.ds(pl.multiple_of(n * 256, 256), 256))
        wat = (pl.ds(pl.multiple_of(n * 256, 256), 256), slice(None))
        d = dss()
        pack(flat, WDN, n * 256, 256, 0, dot3(split2(jnp.transpose(hid[at])), d, NN))
        dh = dot3(d, (wdn[wat], wdnl[wat]), NT)
        p = pre[at]
        th = jnp.tanh(c1 * (p + c2 * (p * p * p)))
        dp = dh * (0.5 * (1.0 + th) + 0.5 * p * (1.0 - th * th) * (c1 * (1.0 + (3.0 * c2) * (p * p))))
        dps = split2(dp)
        pack(flat, WUP, 0, 512, n * 2, dot3(nt, dps, NN))
        return acc + dot3(dps, (wup[at], wupl[at]), NT)
    dn = lax.fori_loop(0, 8, hidden, jnp.zeros((256, 512), jnp.float32))
    ship(1, WDN); ship(2, WUP)
    norm = state[...] * r
    ds = state2[...] + r * (dn - norm * jnp.mean(dn * norm, axis=1, keepdims=True))
    put2((a5, a5l), ds, slice(None), slice(None))
    def gin(n, carry):
        at = (slice(None), pl.ds(pl.multiple_of(n * 256, 256), 256))
        pack(flat, WIN, n * 256, 256, 0, dot3(split2(jnp.transpose(x[at])), (a5[...], a5l[...]), NN))
        return carry
    lax.fori_loop(0, 6, gin, 0)
    ship(3, WIN)
    for c in ships: c.wait()

def learn(got, gathered):
    f32, b16 = jnp.float32, jnp.bfloat16
    V = pltpu.VMEM
    both = lambda *s: [V(s, b16), V(s, b16)]
    return pl.pallas_call(
        learn_kernel,
        out_shape=(jax.ShapeDtypeStruct((256, 1536), f32), jax.ShapeDtypeStruct((28672, 128), f32)),
        in_specs=[pl.BlockSpec(memory_space=pltpu.VMEM), pl.BlockSpec(memory_space=pl.ANY)],
        out_specs=(pl.BlockSpec(memory_space=pltpu.VMEM), pl.BlockSpec(memory_space=pl.ANY)),
        scratch_shapes=[V((28672, 128), f32), V((128, 8, 128), f32)] + both(1536, 512) + both(512, 2048) + both(2048, 512) + both(512, 1536)
            + [V((256, 1536), f32), V((256, 1536), f32)] + both(256, 1536) + [V((256, 2048), f32), V((256, 2048), f32)] + both(256, 512)
            + [V((256, 512), f32), V((256, 512), f32), V((3, 256, 256), b16), pltpu.SemaphoreType.DMA((2,)), pltpu.SemaphoreType.DMA((4,))],
        compiler_params=pltpu.CompilerParams(vmem_limit_bytes=60 << 20),
        name="learn",
    )(got, gathered)

def adam(shard, grad, moment, second):
    new_m = beta_first * moment + (1.0 - beta_first) * grad
    new_v = beta_second * second + (1.0 - beta_second) * grad * grad
    update = (
        new_m
        / (1.0 - beta_first**adam_count)
        / (jnp.sqrt(new_v / (1.0 - beta_second**adam_count)) + adam_epsilon)
    )
    return (shard - learn_rate * update, new_m, new_v)

def local(velocity, viscosity, sample_idx, assign, params, adam_m, adam_v):
    slots = jnp.pad(assign.reshape(2, 128).astype(jnp.float32), ((0, 6), (0, 0)))
    shard = jnp.concatenate([params.reshape(224, 128), slots], axis=0)
    velocity_next, gathered, got = front(shard, velocity, viscosity, assign, sample_idx)
    prediction, grad = learn(got.reshape(6144, 128), gathered.reshape(128, 232, 128))
    mine = reduce_scatter(grad.reshape(2, 2, 2, 4, 4, 224, 128)).reshape(-1)
    new_params, new_m, new_v = adam(params, mine, adam_m, adam_v)
    return (velocity_next, prediction, new_params, new_m, new_v)


def solution(mesh):
    placed = (
        P(None, ("group", "dev"), None, None),
        P(("group", "dev"), None, None),
        P(("group", "dev"), None),
        P(("group", "dev"), None),
        P(("group", "dev")),
        P(("group", "dev")),
        P(("group", "dev")),
    )
    return jax.shard_map(
        local,
        mesh=mesh,
        in_specs=placed,
        out_specs=(
            P(None, ("group", "dev"), None, None),
            P(("group", "dev"), None),
            P(("group", "dev")),
            P(("group", "dev")),
            P(("group", "dev")),
        ),
        check_vma=False,
    )
```

```python
import jax
import jax.numpy as jnp
from jax import lax
from jax.experimental import pallas as pl
from jax.experimental.pallas import tpu as pltpu
from jax.sharding import PartitionSpec as P

time_step = 0.5
norm_epsilon = 1e-06
beta_first = 0.9
beta_second = 0.95
learn_rate = 0.01
adam_epsilon = 1e-08
adam_count = 10

MESH = pl.DeviceIdType.MESH
PIECES = ((0, 72), (72, 80), (152, 72))
ORDERS = ((0, 1, 2), (1, 2, 0), (2, 0, 1))

def coords():
    g = lax.axis_index("group"); d = lax.axis_index("dev")
    return (d % 4, (d // 4) % 4, (g // 2) * 2 + d // 16), g % 2

def ident(xyz, core):
    x, y, z = xyz
    return ((z // 2) * 2 + core, (z % 2) * 16 + y * 4 + x)

def shifted(xyz, axis, by):
    out = list(xyz); out[axis] = (xyz[axis] + by) % 4
    return tuple(out)

def neighbours(xyz, core):
    ids = [ident(shifted(xyz, a, s), core) for a in range(3) for s in (1, 3)]
    return ids + [ident(xyz, 1 - core)]

def region(ref, full, xyz, core, r0, n):
    x = slice(None) if 0 in full else xyz[0]
    y = slice(None) if 1 in full else xyz[1]
    zh = slice(None) if 2 in full else xyz[2] // 2
    zl = slice(None) if 2 in full else xyz[2] % 2
    return ref.at[zh, core, zl, y, x, pl.ds(r0, n), :]

def halves(piece, pieces=PIECES):
    r0, n = pieces[piece]
    n0 = (n // 16) * 8 if n % 16 else n // 2
    return (r0, n0), (r0 + n0, n - n0)


def pick(full, xyz, present=(0, 1, 2)):
    out = []
    if 2 in present: out += [slice(None)] * 2 if 2 in full else [xyz[2] // 2, xyz[2] % 2]
    if 1 in present: out += [slice(None)] if 1 in full else [xyz[1]]
    if 0 in present: out += [slice(None)] if 0 in full else [xyz[0]]
    return tuple(out)

def walk(full, xyz, body):
    full = tuple(full)
    if not full:
        body(xyz); return
    def step(i, carry):
        at = list(xyz)
        for k, a in enumerate(full):
            at[a] = (i // (4 ** k)) % 4
        body(tuple(at)); return carry
    lax.fori_loop(0, 4 ** len(full), step, 0)

def dims(present):
    out = ()
    if 2 in present: out += (2, 2)
    if 1 in present: out += (4,)
    if 0 in present: out += (4,)
    return out


def advance_planes(ext, visc, start, stop, store):
    def body(x, carry):
        mid = [ext[c, x + 1] for c in range(3)]
        nu = visc[x]
        new = []
        for c in range(3):
            up1, lo1 = ext[c, x + 2], ext[c, x]
            up2, lo2 = pltpu.roll(mid[c], 127, 0), pltpu.roll(mid[c], 1, 0)
            up3, lo3 = pltpu.roll(mid[c], 127, 1), pltpu.roll(mid[c], 1, 1)
            laplace = up1 + lo1 + up2 + lo2 + up3 + lo3 - 6.0 * mid[c]
            advect = 0.5 * (mid[0] * (up1 - lo1) + mid[1] * (up2 - lo2) + mid[2] * (up3 - lo3))
            new.append(mid[c] + time_step * (nu * laplace - advect))
        store(x, new)
        return carry
    lax.fori_loop(start, stop, body, 0)

def split3(x):
    high = x.astype(jnp.bfloat16); rest = x - high.astype(jnp.float32)
    mid = rest.astype(jnp.bfloat16)
    low = (rest - mid.astype(jnp.float32)).astype(jnp.bfloat16)
    return high, mid, low

def permuted(onehot, x):
    n = x.shape[1]
    parts = jnp.dot(onehot, jnp.concatenate(split3(x), axis=1), preferred_element_type=jnp.float32)
    return parts[:, :n] + parts[:, n:2 * n] + parts[:, 2 * n:]

def swap_groups(x):
    row = lax.broadcasted_iota(jnp.int32, x.shape, 0)
    lane = lax.broadcasted_iota(jnp.int32, x.shape, 1)
    for b in range(4):
        k = 1 << b
        rb, lb = (row >> b) & 1, (lane >> (3 + b)) & 1
        above = pltpu.roll(pltpu.roll(x, 256 - k, 0), 8 * k, 1)
        below = pltpu.roll(pltpu.roll(x, k, 0), 128 - 8 * k, 1)
        x = jnp.where(rb == lb, x, jnp.where(rb == 0, above, below))
    return x

def send_order(assign, sample):
    target = assign // 256
    column = jnp.transpose(jnp.broadcast_to(target, (128, 256)))[:, :1]
    before = lax.broadcasted_iota(jnp.int32, (256, 256), 0) < lax.broadcasted_iota(jnp.int32, (256, 256), 1)
    same = jnp.where((column == target) & before, 1, 0)
    rank = jnp.sum(same, axis=0, keepdims=True)
    dst = lax.broadcasted_iota(jnp.int32, (128, 256), 0)
    rows = [jnp.where((target == dst) & (rank == j), 1.0, 0.0) for j in range(2)]
    chosen = jnp.concatenate(rows, axis=0).astype(jnp.bfloat16)
    patch = jnp.where(sample == lax.broadcasted_iota(jnp.int32, (256, 256), 0), 1.0, 0.0).astype(jnp.bfloat16)
    return lax.dot_general(chosen, patch, (((1,), (1,)), ((), ())), preferred_element_type=jnp.float32).astype(jnp.bfloat16)

GATHER = ((0, 72), (72, 80), (152, 80))

def front_kernel(shard, vel, visc, assign, sample, nxt, out, got, ext, vext, first, order, s0, *rest):
    s1, s2, s3, relay = rest[0:3], rest[3:6], rest[6:9], rest[9:27]
    hs, hr, lsem, ssem, rsem, cs, cr, xs, xr, xl = rest[27:]
    xyz, core = coords()
    me = lax.axis_index("group") * 32 + lax.axis_index("dev")
    after, before = (me + 1) % 128, (me + 127) % 128
    after_id, before_id = (after // 32, after % 32), (before // 32, before % 32)
    own = pltpu.make_async_copy(shard, out.at[xyz[2] // 2, core, xyz[2] % 2, xyz[1], xyz[0]], lsem)
    own.start()
    barrier = pltpu.get_barrier_semaphore()
    ids = neighbours(xyz, core) + [ident(shifted(xyz, a, 2), core) for a in range(3)] + [after_id, before_id]
    for i in ids:
        pl.semaphore_signal(barrier, inc=1, device_id=i, device_id_type=MESH)
    ext[:, 2:10] = vel[...]
    vext[1:9] = visc[...]
    pl.semaphore_wait(barrier, len(ids))
    sib = ident(xyz, 1 - core)
    pend = []

    def remote(src, dst, s, r, to):
        c = pltpu.make_async_remote_copy(src_ref=src, dst_ref=dst, send_sem=s, recv_sem=r, device_id=to, device_id_type=MESH)
        c.start(); pend.append(c)
        return c

    sibs = []
    def to_sib(src):
        k = len(sibs)
        sibs.append(remote(src, src, cs.at[k], cr.at[k], sib))
    steps = {}
    def around(p, phase):
        a = ORDERS[p][phase]; full = ORDERS[p][:phase]
        at = [shifted(xyz, a, k) for k in range(4)]
        return full, at, ident(at[1], core), ident(at[3], core), halves(p, GATHER), (phase * 3 + p) * 6, GATHER[p]
    def g_send(p, phase, kind, at, half, to):
        full, _, _, _, hs_, base, _ = around(p, phase)
        r0, n = hs_[half]
        src = region(out, full, at, core, r0, n)
        steps[p, phase, kind] = remote(src, src, ssem.at[base + kind], rsem.at[base + kind], to)
    def g_start(phase):
        for p in range(3):
            full, at, R, L, hv, base, (r0, n) = around(p, phase)
            if phase == 0:
                src = region(out, full, at[0], core, r0, n)
                for kind, k in ((2, 2), (0, 1), (3, 3)):
                    steps[p, 0, kind] = remote(src, src, ssem.at[base + kind], rsem.at[base + kind], ident(at[k], core))
                continue
            g_send(p, phase, 0, at[0], 0, R)
            g_send(p, phase, 3, at[0], 1, L)
            g_send(p, phase, 1, at[0], 1, R)
            g_send(p, phase, 4, at[0], 0, L)
            if phase == 2: to_sib(region(out, full, at[0], core, r0, n))
    def g_forward(phase):
        for p in range(3):
            full, at, R, L, hv, base, _ = around(p, phase)
            steps[p, phase, 0].wait_recv(); g_send(p, phase, 2, at[3], 0, R)
            steps[p, phase, 3].wait_recv(); g_send(p, phase, 5, at[1], 1, L)
    def g_near(phase):
        for p in range(3):
            full, at, R, L, hv, base, (r0, n) = around(p, phase)
            steps[p, phase, 1].wait_recv(); steps[p, phase, 4].wait_recv()
            if phase == 2:
                to_sib(region(out, full, at[3], core, r0, n))
                to_sib(region(out, full, at[1], core, r0, n))
    def g_far(phase):
        for p in range(3):
            full, at, R, L, hv, base, (r0, n) = around(p, phase)
            steps[p, phase, 2].wait_recv(); steps[p, phase, 5].wait_recv()
            if phase == 2: to_sib(region(out, full, at[2], core, r0, n))

    moves, selfs = {}, {}
    def x_core():
        blocks = s0.reshape(2, 2, 2, 4, 4, 48, 128)
        for p in range(3):
            for zh in range(2):
                k = p * 2 + zh
                rows = pl.ds(16 * p, 16)
                moves[p, 0, zh] = remote(blocks.at[zh, 1 - core, :, :, :, rows], s1[p].at[core, zh], xs.at[k], xr.at[k], sib)
                selfs[p, 0, zh] = pltpu.make_async_copy(blocks.at[zh, core, :, :, :, rows], s1[p].at[core, zh], xl.at[k])
                selfs[p, 0, zh].start()
    def stage(p, s):
        a = ORDERS[p][s - 1]; others = ORDERS[p][s:]
        src = (s1, s2, s3)[s - 1][p]
        dst = got.at[p] if s == 3 else (s2, s3)[s - 1][p]
        at = [shifted(xyz, a, k) for k in range(4)]
        left = (slice(None),) * s
        def part(k, r0, n): return src.at[left + pick(others, at[k], (a,) + others) + (pl.ds(r0, n),)]
        free = (slice(None),) * (s + len(dims(others)))
        def land(k, r0, n): return dst.at[(at[k][a],) + free + (pl.ds(r0, n),)]
        return part, land, ident(at[1], core), ident(at[3], core), 6 + ((s - 1) * 3 + p) * 6
    def x_start(s):
        for p in range(3):
            part, land, R, L, base = stage(p, s)
            if s == 1:
                for zh in range(2): moves[p, 0, zh].wait_recv(); selfs[p, 0, zh].wait()
            else:
                for k in (0, 1, 4, 5): moves[p, s - 1, k].wait_recv()
                selfs[p, s - 1].wait()
            def mv(k, src, dst, to): moves[p, s, k] = remote(src, dst, xs.at[base + k], xr.at[base + k], to)
            via = relay[((s - 1) * 3 + p) * 2], relay[((s - 1) * 3 + p) * 2 + 1]
            mv(2, part(2, 0, 8), via[0], R)
            mv(3, part(2, 8, 8), via[1], L)
            mv(0, part(1, 0, 16), land(0, 0, 16), R)
            mv(1, part(3, 0, 16), land(0, 0, 16), L)
            c = pltpu.make_async_copy(part(0, 0, 16), land(0, 0, 16), xl.at[6 + (s - 1) * 3 + p])
            c.start(); selfs[p, s] = c
    def x_relay(s):
        for p in range(3):
            part, land, R, L, base = stage(p, s)
            via = relay[((s - 1) * 3 + p) * 2], relay[((s - 1) * 3 + p) * 2 + 1]
            moves[p, s, 2].wait_recv()
            moves[p, s, 4] = remote(via[0], land(3, 0, 8), xs.at[base + 4], xr.at[base + 4], R)
            moves[p, s, 3].wait_recv()
            moves[p, s, 5] = remote(via[1], land(1, 8, 8), xs.at[base + 5], xr.at[base + 5], L)
    def x_finish():
        for p in range(3):
            for k in (0, 1, 4, 5): moves[p, 3, k].wait_recv()
            selfs[p, 3].wait()

    def put_first(x, new):
        for c in range(3): first[c, x] = new[c]
    def put_next(x, new):
        for c in range(3): nxt[c, x] = new[c]
    own.wait()
    g_start(0)
    halo = [remote(vel.at[:, 6:8], ext.at[:, 0:2], hs.at[0], hr.at[0], after_id),
            remote(vel.at[:, 0:2], ext.at[:, 10:12], hs.at[1], hr.at[1], before_id),
            remote(visc.at[7:8], vext.at[0:1], hs.at[2], hr.at[2], after_id),
            remote(visc.at[0:1], vext.at[9:10], hs.at[3], hr.at[3], before_id)]
    order[...] = send_order(assign[...], sample[...])
    advance_planes(ext, vext, 2, 8, put_first)
    for p in range(3):
        for kind in (0, 2, 3): steps[p, 0, kind].wait_recv()
    g_start(1)
    for c in halo: c.wait_recv()
    lower = jnp.where(me > 0, 1.0, 0.0); upper = jnp.where(me < 127, 1.0, 0.0)
    ext[:, 0:2] = ext[:, 0:2] * lower
    vext[0:1] = vext[0:1] * lower
    ext[:, 10:12] = ext[:, 10:12] * upper
    vext[9:10] = vext[9:10] * upper
    advance_planes(ext, vext, 0, 2, put_first)
    advance_planes(ext, vext, 8, 10, put_first)
    g_forward(1)
    advance_planes(first, visc, 0, 8, put_next)
    g_near(1); g_far(1)
    g_start(2)
    def body(i, carry):
        c, q = i // 4, i % 4
        for field, ref, off in ((0, first, 1), (1, nxt, 0)):
            a, b = ref[c, 2 * q + off], ref[c, 2 * q + off + 1]
            pieces = []
            for iy in range(16):
                pieces += [a[iy * 8:iy * 8 + 8], b[iy * 8:iy * 8 + 8]]
            res = permuted(order[...], swap_groups(jnp.concatenate(pieces, axis=0)))
            for j in range(2):
                s0[pl.ds(j * 24 + field * 12 + i, 128, stride=48), :] = res[j * 128:(j + 1) * 128]
        return carry
    lax.fori_loop(0, 12, body, 0)
    x_core()
    g_forward(2)
    x_start(1)
    g_near(2)
    x_relay(1)
    x_start(2)
    g_far(2)
    x_relay(2)
    x_start(3)
    x_relay(3)
    x_finish()
    for c in sibs: c.wait_recv()
    for c in pend: c.wait_send()

def front(shard, vel, visc, assign, sample):
    f32, V = jnp.float32, pltpu.VMEM
    scratch = [V((3, 12, 128, 128), f32), V((10, 128, 128), f32), V((3, 10, 128, 128), f32), V((256, 256), jnp.bfloat16), V((6144, 128), f32)]
    scratch += [V((2, 2, 2, 4, 4, 16, 128), f32)] * 3
    for s in (2, 3):
        for p in range(3):
            scratch.append(V((4,) * (s - 1) + (2,) + dims(ORDERS[p][s - 1:]) + (16, 128), f32))
    for s in (1, 2, 3):
        for p in range(3):
            scratch += [V((4,) * (s - 1) + (2,) + dims(ORDERS[p][s:]) + (8, 128), f32)] * 2
    D = pltpu.SemaphoreType.DMA
    scratch += [D((4,)), D((4,)), D, D((54,)), D((54,)), D((12,)), D((12,)), D((60,)), D((60,)), D((15,))]
    A = pl.BlockSpec(memory_space=pl.ANY); M = pl.BlockSpec(memory_space=pltpu.VMEM)
    return pl.pallas_call(
        front_kernel,
        out_shape=(jax.ShapeDtypeStruct((3, 8, 128, 128), f32), jax.ShapeDtypeStruct((2, 2, 2, 4, 4, 232, 128), f32),
                   jax.ShapeDtypeStruct((3, 4, 4, 4, 2, 16, 128), f32)),
        in_specs=[A, M, M, M, M], out_specs=(M, A, A), scratch_shapes=scratch,
        compiler_params=pltpu.CompilerParams(collective_id=0, has_side_effects=True, vmem_limit_bytes=58 << 20),
        name="front",
    )(shard, vel, visc, assign, sample)

BLOCK = 232
WIN, WUP, WDN, WOUT = (0, 1536, 4), (6144, 512, 16), (14336, 2048, 4), (22528, 512, 12)
NN = (((1,), (0,)), ((), ())); NT = (((1,), (1,)), ((), ()))

def split2(x):
    high = x.astype(jnp.bfloat16)
    return high, (x - high.astype(jnp.float32)).astype(jnp.bfloat16)

def dot3(a, b, form):
    d = lambda p, q: lax.dot_general(p, q, form, preferred_element_type=jnp.float32)
    return d(a[0], b[0]) + (d(a[0], b[1]) + d(a[1], b[0]))

def put2(refs, value, *at):
    for r, v in zip(refs, split2(value)): r[at] = v

def unpack(flat, spec, hi, lo):
    base, rows, cols = spec
    n = 256
    def body(i, carry):
        for q in range(cols):
            start = base + i * (n * cols) + q
            h, l = split2(flat[pl.ds(start, n, stride=cols), :])
            at = (pl.ds(pl.multiple_of(i * n, n), n), pl.ds(q * 128, 128))
            hi[at] = h; lo[at] = l
        return carry
    lax.fori_loop(0, rows // n, body, 0)

def pack(flat, spec, r0, n, c0, value):
    base, rows, cols = spec
    for q in range(value.shape[1] // 128):
        flat[pl.ds(base + r0 * cols + c0 + q, n, stride=cols), :] = value[:, q * 128:(q + 1) * 128]

def slot_matrices(assign, me):
    mine = (assign // 256) == me
    t = lax.broadcasted_iota(jnp.int32, (128, 256), 1)
    first = jnp.min(jnp.where(mine, t, 512), axis=1, keepdims=True)
    last = jnp.max(jnp.where(mine, t, -1), axis=1, keepdims=True)
    slot = assign % 256
    cols = [jnp.sum(jnp.where(t == at, slot, 0), axis=1, keepdims=True) for at in (first, last)]
    want = [jnp.where(c == t, 1.0, 0.0).astype(jnp.bfloat16) for c in cols]
    k = lax.broadcasted_iota(jnp.int32, (128, 128), 0)
    src = lax.broadcasted_iota(jnp.int32, (128, 128), 1)
    moved = []
    for p in range(3):
        co = {ORDERS[p][2]: k // 32, ORDERS[p][1]: (k // 8) % 4, ORDERS[p][0]: (k // 2) % 4}
        flat = (co[2] // 2) * 64 + (k % 2) * 32 + (co[2] % 2) * 16 + co[1] * 4 + co[0]
        perm = jnp.where(flat == src, 1.0, 0.0).astype(jnp.bfloat16)
        moved.append([jnp.dot(perm, w, preferred_element_type=jnp.float32) for w in want])
    return [jnp.transpose(jnp.concatenate([moved[p0][0], moved[p1][1]], axis=0)).astype(jnp.bfloat16) for p0, p1 in PAIRS]

PAIRS = ((0, 1), (0, 2), (1, 2))

def back_kernel(got, gathered, pred, mine, flat, asg, win, winl, wup, wupl, wdn, wdnl, wout, woutl,
                 x, tgt, xs, xsl, hid, pre, a5, a5l, state, state2, rowsc, crecv, *rest):
    bufs, (sem, cs, cr, ssem, rsem) = rest[:33], rest[33:]
    me = lax.axis_index("group") * 32 + lax.axis_index("dev")
    xyz, core = coords()
    barrier = pltpu.get_barrier_semaphore()
    ids = neighbours(xyz, core) + [ident(shifted(xyz, a, 2), core) for a in range(3)]
    for i in ids:
        pl.semaphore_signal(barrier, inc=1, device_id=i, device_id_type=MESH)
    ac = pltpu.make_async_copy(gathered.at[:, pl.ds(224, 8), :], asg, sem.at[0])
    wc = pltpu.make_async_copy(gathered.at[:, pl.ds(0, 224), :], flat.reshape(128, 224, 128), sem.at[1])
    ac.start(); wc.start()
    ac.wait()
    assign = jnp.concatenate([asg[:, 0, :], asg[:, 1, :]], axis=1).astype(jnp.int32)
    for i, place in enumerate(slot_matrices(assign, me)): rowsc[i] = place
    for field, ref in ((0, x), (1, tgt)):
        for k in range(12):
            col = [j * 24 + field * 12 + k for j in range(2)]
            src = jnp.concatenate([got[pl.ds((c // 16) * 2048 + c % 16, 128, stride=16), :] for c in col], axis=0)
            ref[:, k * 128:(k + 1) * 128] = permuted(rowsc[(col[0]) // 8], src)
    wc.wait()
    unpack(flat, WIN, win, winl)
    unpack(flat, WUP, wup, wupl)
    unpack(flat, WDN, wdn, wdnl)
    unpack(flat, WOUT, wout, woutl)
    put2((xs, xsl), x[...], slice(None), slice(None))
    for n in range(2):
        at = (slice(None), pl.ds(n * 256, 256))
        state[at] = dot3((xs[...], xsl[...]), (win[at], winl[at]), NN)
    s = state[...]
    r = lax.rsqrt(jnp.mean(s * s, axis=1, keepdims=True) + norm_epsilon)
    put2((a5, a5l), s * r, slice(None), slice(None))
    c1, c2 = 0.7978845608028654, 0.044715
    def up(n, carry):
        at = (slice(None), pl.ds(pl.multiple_of(n * 256, 256), 256))
        p = dot3((a5[...], a5l[...]), (wup[at], wupl[at]), NN)
        pre[at] = p
        hid[at] = 0.5 * p * (1.0 + jnp.tanh(c1 * (p + c2 * (p * p * p))))
        return carry
    lax.fori_loop(0, 8, up, 0)
    def down(n, acc):
        at = (slice(None), pl.ds(pl.multiple_of(n * 256, 256), 256))
        wat = (pl.ds(pl.multiple_of(n * 256, 256), 256), slice(None))
        return acc + dot3(split2(hid[at]), (wdn[wat], wdnl[wat]), NN)
    state2[...] = lax.fori_loop(0, 8, down, s)
    s2 = split2(state2[...])
    def outp(n, carry):
        at = (slice(None), pl.ds(pl.multiple_of(n * 256, 256), 256))
        g = x[at] + dot3(s2, (wout[at], woutl[at]), NN)
        pred[at] = g
        tgt[at] = (g - tgt[at]) * (1.0 / 256.0)
        return carry
    lax.fori_loop(0, 6, outp, 0)
    blocks = flat.reshape(2, 2, 2, 4, 4, 224, 128)
    sib = ident(xyz, 1 - core)
    def swap(n):
        src, dst = (blocks.at[1, 1 - core], crecv.at[1]) if n == 0 else (blocks.at[0, 1 - core, n - 1], crecv.at[0, n - 1])
        return pltpu.make_async_remote_copy(src_ref=src, dst_ref=dst, send_sem=cs.at[n], recv_sem=cr.at[n], device_id=sib, device_id_type=MESH)
    def swap_add(n):
        swap(n).wait_recv()
        def body(i, carry):
            at = ((1, i // 16) if n == 0 else (0, n - 1)) + ((i // 4) % 4, i % 4)
            mineat = (at[0], core) + at[1:]
            blocks[mineat] = blocks[mineat] + crecv[at]
            return carry
        lax.fori_loop(0, 32 if n == 0 else 16, body, 0)
    s2t = split2(jnp.transpose(state2[...]))
    def gout(n, acc):
        at = (slice(None), pl.ds(pl.multiple_of(n * 256, 256), 256))
        e = split2(tgt[at])
        pack(flat, WOUT, 0, 512, n * 2, dot3(s2t, e, NN))
        return acc + dot3(e, (wout[at], woutl[at]), NT)
    ds2 = lax.fori_loop(0, 6, gout, jnp.zeros((256, 512), jnp.float32))
    state2[...] = ds2
    put2((xs, xsl), ds2, slice(None), pl.ds(0, 512))
    dss = lambda: (xs[:, :512], xsl[:, :512])
    normt = jnp.transpose(state[...] * r)
    nt = split2(normt)
    def gdown(n, carry):
        at = (slice(None), pl.ds(pl.multiple_of(n * 256, 256), 256))
        pack(flat, WDN, n * 256, 256, 0, dot3(split2(jnp.transpose(hid[at])), dss(), NN))
        return carry
    lax.fori_loop(0, 8, gdown, 0)
    pl.semaphore_wait(barrier, len(ids))
    swap(0).start()
    def hidden(n, acc):
        at = (slice(None), pl.ds(pl.multiple_of(n * 256, 256), 256))
        wat = (pl.ds(pl.multiple_of(n * 256, 256), 256), slice(None))
        dh = dot3(dss(), (wdn[wat], wdnl[wat]), NT)
        p = pre[at]
        th = jnp.tanh(c1 * (p + c2 * (p * p * p)))
        dp = dh * (0.5 * (1.0 + th) + 0.5 * p * (1.0 - th * th) * (c1 * (1.0 + (3.0 * c2) * (p * p))))
        dps = split2(dp)
        pack(flat, WUP, 0, 512, n * 2, dot3(nt, dps, NN))
        return acc + dot3(dps, (wup[at], wupl[at]), NT)
    pend = []
    first, second, third = big_phase(blocks, bufs, ssem, rsem, xyz, core, pend)
    lower, upper = (0, 1, 2), (3, 4)
    dn = lax.fori_loop(0, 4, hidden, jnp.zeros((256, 512), jnp.float32))
    swap_add(0)
    first(upper)
    dn = lax.fori_loop(4, 8, hidden, dn)
    @pl.when(core == 0)
    def _():
        swap(1).start()
        swap(2).start()
    second(upper)
    norm = state[...] * r
    ds = state2[...] + r * (dn - norm * jnp.mean(dn * norm, axis=1, keepdims=True))
    put2((a5, a5l), ds, slice(None), slice(None))
    def gin(n, carry):
        at = (slice(None), pl.ds(pl.multiple_of(n * 256, 256), 256))
        pack(flat, WIN, n * 256, 256, 0, dot3(split2(jnp.transpose(x[at])), (a5[...], a5l[...]), NN))
        return carry
    lax.fori_loop(0, 4, gin, 0)
    @pl.when(core == 1)
    def _(): swap(1).start()
    lax.fori_loop(4, 6, gin, 0)
    @pl.when(core == 1)
    def _(): swap(2).start()
    swap_add(1)
    swap_add(2)
    first(lower)
    third(upper)
    second(lower)
    third(lower)
    small_phases(blocks, mine, bufs[12:], ssem, rsem, xyz, core, pend)
    for c in pend: c.wait_send()
    for n in range(3): swap(n).wait_send()

SPREAD = ((0, 48), (48, 88), (136, 88))
UNITS = ((0, None), (1, 0), (2, 0), (1, 1), (2, 1))

def place(full, at, core, r0, n, half=None):
    i = pick(full, at)
    if half is not None: i = (half,) + i[1:]
    return (i[0], core) + i[1:] + (pl.ds(r0, n), slice(None))

def walk_half(full, xyz, half, body):
    sizes = [2 if a == 2 and half is not None else 4 for a in full]
    count = 1
    for n in sizes: count *= n
    def step(i, carry):
        at = list(xyz)
        for a, n in zip(full, sizes):
            at[a] = i % n + (2 * half if n == 2 else 0)
            i = i // n
        body(tuple(at)); return carry
    lax.fori_loop(0, count, step, 0)

def big_phase(blocks, bufs, ssem, rsem, xyz, core, pend):
    copies = {}
    def of(u):
        p, half = UNITS[u]; a = ORDERS[p][2]; full = ORDERS[p][:2]
        ids = [ident(shifted(xyz, a, k), core) for k in range(4)]
        refs = [b if half is None else b.at[half] for b in bufs[p * 4:p * 4 + 4]]
        lead = (slice(None),) * (len(dims(full)) - (half is not None))
        return p, half, a, full, ids, refs, lead
    def send(u, kind, rel, r0, n, to, dst):
        p, half, a, full, ids, _, _ = of(u)
        c = pltpu.make_async_remote_copy(src_ref=blocks.at[place(full, shifted(xyz, a, rel), core, r0, n, half)], dst_ref=dst,
            send_sem=ssem.at[u * 6 + kind], recv_sem=rsem.at[u * 6 + kind], device_id=ids[to], device_id_type=MESH)
        c.start(); copies[u, kind] = c; pend.append(c)
    def fold(u, kind, rel, r0, n, slot, off):
        p, half, a, full, _, _, _ = of(u)
        copies[u, kind].wait_recv()
        ref = bufs[p * 4 + slot]
        def body(at):
            i = place((), at, core, r0, n)
            blocks[i] = blocks[i] + ref[pick((), at, full) + (pl.ds(off, n), slice(None))]
        walk_half(full, shifted(xyz, a, rel), half, body)
    def first(units):
        for u in units:
            p, _, _, _, _, refs, lead = of(u)
            (h0, n0), (h1, n1) = halves(p, SPREAD)
            send(u, 0, 2, h0, n0, 1, refs[0])
            send(u, 3, 2, h1, n1, 3, refs[1])
        for u in units:
            p, _, _, _, _, refs, lead = of(u)
            (h0, n0), (h1, n1) = halves(p, SPREAD)
            send(u, 1, 1, h1, n1, 1, refs[2].at[lead + (pl.ds(n0, n1),)])
            send(u, 4, 3, h0, n0, 3, refs[3].at[lead + (pl.ds(0, n0),)])
    def second(units):
        for u in units:
            p, _, _, _, _, refs, lead = of(u)
            (h0, n0), (h1, n1) = halves(p, SPREAD)
            fold(u, 0, 1, h0, n0, 0, 0); send(u, 2, 1, h0, n0, 1, refs[2].at[lead + (pl.ds(0, n0),)])
            fold(u, 3, 3, h1, n1, 1, 0); send(u, 5, 3, h1, n1, 3, refs[3].at[lead + (pl.ds(n0, n1),)])
    def third(units):
        for u in units:
            (h0, n0), (h1, n1) = halves(UNITS[u][0], SPREAD)
            fold(u, 1, 0, h1, n1, 2, n0); fold(u, 4, 0, h0, n0, 3, 0)
        for u in units:
            (h0, n0), (h1, n1) = halves(UNITS[u][0], SPREAD)
            fold(u, 2, 0, h0, n0, 2, 0); fold(u, 5, 0, h1, n1, 3, n0)
    return first, second, third

def small_phases(blocks, mine, bufs, ssem, rsem, xyz, core, pend):
    copies = {}
    def send(p, phase, kind, rel, r0, n, to, dst):
        a = ORDERS[p][2 - phase]; full = ORDERS[p][:2 - phase]
        k = 30 + ((phase - 1) * 3 + p) * 6 + kind
        c = pltpu.make_async_remote_copy(src_ref=blocks.at[place(full, shifted(xyz, a, rel), core, r0, n)], dst_ref=dst,
            send_sem=ssem.at[k], recv_sem=rsem.at[k], device_id=ident(shifted(xyz, a, to), core), device_id_type=MESH)
        c.start(); copies[p, phase, kind] = c; pend.append(c)
    def fold(p, phase, kind, rel, r0, n, ref, off):
        a = ORDERS[p][2 - phase]; full = ORDERS[p][:2 - phase]
        copies[p, phase, kind].wait_recv()
        def body(at):
            i = place((), at, core, r0, n)
            blocks[i] = blocks[i] + ref[pick((), at, full) + (pl.ds(off, n), slice(None))]
        walk(full, shifted(xyz, a, rel), body)
    for p in range(3):
        b = bufs[p * 4:p * 4 + 4]; (h0, n0), (h1, n1) = halves(p, SPREAD)
        lead = (slice(None),) * len(dims(ORDERS[p][:1]))
        send(p, 1, 0, 2, h0, n0, 1, b[0])
        send(p, 1, 3, 2, h1, n1, 3, b[1])
        send(p, 1, 1, 1, h1, n1, 1, b[2].at[lead + (pl.ds(n0, n1),)])
        send(p, 1, 4, 3, h0, n0, 3, b[3].at[lead + (pl.ds(0, n0),)])
    for p in range(3):
        b = bufs[p * 4:p * 4 + 4]; (h0, n0), (h1, n1) = halves(p, SPREAD)
        lead = (slice(None),) * len(dims(ORDERS[p][:1]))
        fold(p, 1, 0, 1, h0, n0, b[0], 0); send(p, 1, 2, 1, h0, n0, 1, b[2].at[lead + (pl.ds(0, n0),)])
        fold(p, 1, 3, 3, h1, n1, b[1], 0); send(p, 1, 5, 3, h1, n1, 3, b[3].at[lead + (pl.ds(n0, n1),)])
    for p in range(3):
        b = bufs[p * 4:p * 4 + 4]; (h0, n0), (h1, n1) = halves(p, SPREAD)
        fold(p, 1, 1, 0, h1, n1, b[2], n0); fold(p, 1, 4, 0, h0, n0, b[3], 0)
    for p in range(3):
        b = bufs[p * 4:p * 4 + 4]; (h0, n0), (h1, n1) = halves(p, SPREAD)
        fold(p, 1, 2, 0, h0, n0, b[2], 0); fold(p, 1, 5, 0, h1, n1, b[3], n0)
        b = bufs[12 + p * 3:15 + p * 3]; r0, n = SPREAD[p]
        send(p, 2, 0, 2, r0, n, 2, b[2])
        send(p, 2, 1, 1, r0, n, 1, b[0])
        send(p, 2, 2, 3, r0, n, 3, b[1])
    for p in range(3):
        b = bufs[12 + p * 3:15 + p * 3]; r0, n = SPREAD[p]
        fold(p, 2, 0, 0, r0, n, b[2], 0); fold(p, 2, 1, 0, r0, n, b[0], 0); fold(p, 2, 2, 0, r0, n, b[1], 0)
    mine[...] = blocks[(xyz[2] // 2, core, xyz[2] % 2, xyz[1], xyz[0])]

def back(got, gathered):
    f32, b16 = jnp.float32, jnp.bfloat16
    V = pltpu.VMEM
    both = lambda *s: [V(s, b16), V(s, b16)]
    slots = []
    for phase in range(2):
        for p in range(3):
            lead = dims(ORDERS[p][:2 - phase]); (_, n0), (_, n1) = halves(p, SPREAD)
            slots += [V(lead + (n, 128), f32) for n in (n0, n1, n0 + n1, n0 + n1)]
    for p in range(3): slots += [V((SPREAD[p][1], 128), f32)] * 3
    return pl.pallas_call(
        back_kernel,
        out_shape=(jax.ShapeDtypeStruct((256, 1536), f32), jax.ShapeDtypeStruct((224, 128), f32)),
        in_specs=[pl.BlockSpec(memory_space=pltpu.VMEM), pl.BlockSpec(memory_space=pl.ANY)],
        out_specs=(pl.BlockSpec(memory_space=pltpu.VMEM), pl.BlockSpec(memory_space=pltpu.VMEM)),
        scratch_shapes=[V((28672, 128), f32), V((128, 8, 128), f32)] + both(1536, 512) + both(512, 2048) + both(2048, 512) + both(512, 1536)
            + [V((256, 1536), f32), V((256, 1536), f32)] + both(256, 1536) + [V((256, 2048), f32), V((256, 2048), f32)] + both(256, 512)
            + [V((256, 512), f32), V((256, 512), f32), V((3, 256, 256), b16), V((2, 2, 4, 4, 224, 128), f32)] + slots
            + [pltpu.SemaphoreType.DMA((n,)) for n in (2, 3, 3, 66, 66)],
        compiler_params=pltpu.CompilerParams(collective_id=1, has_side_effects=True, vmem_limit_bytes=61 << 20),
        name="back",
    )(got, gathered)

def adam(shard, grad, moment, second):
    new_m = beta_first * moment + (1.0 - beta_first) * grad
    new_v = beta_second * second + (1.0 - beta_second) * grad * grad
    update = (
        new_m
        / (1.0 - beta_first**adam_count)
        / (jnp.sqrt(new_v / (1.0 - beta_second**adam_count)) + adam_epsilon)
    )
    return (shard - learn_rate * update, new_m, new_v)

def local(velocity, viscosity, sample_idx, assign, params, adam_m, adam_v):
    slots = jnp.pad(assign.reshape(2, 128).astype(jnp.float32), ((0, 6), (0, 0)))
    shard = jnp.concatenate([params.reshape(224, 128), slots], axis=0)
    velocity_next, gathered, got = front(shard, velocity, viscosity, assign, sample_idx)
    prediction, grad = back(got.reshape(6144, 128), gathered.reshape(128, 232, 128))
    new_params, new_m, new_v = adam(params, grad.reshape(-1), adam_m, adam_v)
    return (velocity_next, prediction, new_params, new_m, new_v)


def solution(mesh):
    placed = (
        P(None, ("group", "dev"), None, None),
        P(("group", "dev"), None, None),
        P(("group", "dev"), None),
        P(("group", "dev"), None),
        P(("group", "dev")),
        P(("group", "dev")),
        P(("group", "dev")),
    )
    return jax.shard_map(
        local,
        mesh=mesh,
        in_specs=placed,
        out_specs=(
            P(None, ("group", "dev"), None, None),
            P(("group", "dev"), None),
            P(("group", "dev")),
            P(("group", "dev")),
            P(("group", "dev")),
        ),
        check_vma=False,
    )
```

```python
import jax
import jax.numpy as jnp
from jax import lax
from jax.experimental import pallas as pl
from jax.experimental.pallas import tpu as pltpu
from jax.sharding import PartitionSpec as P

time_step = 0.5
norm_epsilon = 1e-06
beta_first = 0.9
beta_second = 0.95
learn_rate = 0.01
adam_epsilon = 1e-08
adam_count = 10

MESH = pl.DeviceIdType.MESH
PIECES = ((0, 72), (72, 80), (152, 72))
ORDERS = ((0, 1, 2), (1, 2, 0), (2, 0, 1))

def coords():
    g = lax.axis_index("group"); d = lax.axis_index("dev")
    return (d % 4, (d // 4) % 4, (g // 2) * 2 + d // 16), g % 2

def ident(xyz, core):
    x, y, z = xyz
    return ((z // 2) * 2 + core, (z % 2) * 16 + y * 4 + x)

def shifted(xyz, axis, by):
    out = list(xyz); out[axis] = (xyz[axis] + by) % 4
    return tuple(out)

def neighbours(xyz, core):
    ids = [ident(shifted(xyz, a, s), core) for a in range(3) for s in (1, 3)]
    return ids + [ident(xyz, 1 - core)]

def region(ref, full, xyz, core, r0, n):
    x = slice(None) if 0 in full else xyz[0]
    y = slice(None) if 1 in full else xyz[1]
    zh = slice(None) if 2 in full else xyz[2] // 2
    zl = slice(None) if 2 in full else xyz[2] % 2
    return ref.at[zh, core, zl, y, x, pl.ds(r0, n), :]

def halves(piece, pieces=PIECES):
    r0, n = pieces[piece]
    n0 = (n // 16) * 8 if n % 16 else n // 2
    return (r0, n0), (r0 + n0, n - n0)


def pick(full, xyz, present=(0, 1, 2)):
    out = []
    if 2 in present: out += [slice(None)] * 2 if 2 in full else [xyz[2] // 2, xyz[2] % 2]
    if 1 in present: out += [slice(None)] if 1 in full else [xyz[1]]
    if 0 in present: out += [slice(None)] if 0 in full else [xyz[0]]
    return tuple(out)

def walk(full, xyz, body):
    full = tuple(full)
    if not full:
        body(xyz); return
    def step(i, carry):
        at = list(xyz)
        for k, a in enumerate(full):
            at[a] = (i // (4 ** k)) % 4
        body(tuple(at)); return carry
    lax.fori_loop(0, 4 ** len(full), step, 0)

def dims(present):
    out = ()
    if 2 in present: out += (2, 2)
    if 1 in present: out += (4,)
    if 0 in present: out += (4,)
    return out


def advance_planes(ext, visc, start, stop, store):
    def body(x, carry):
        mid = [ext[c, x + 1] for c in range(3)]
        nu = visc[x]
        new = []
        for c in range(3):
            up1, lo1 = ext[c, x + 2], ext[c, x]
            up2, lo2 = pltpu.roll(mid[c], 127, 0), pltpu.roll(mid[c], 1, 0)
            up3, lo3 = pltpu.roll(mid[c], 127, 1), pltpu.roll(mid[c], 1, 1)
            laplace = up1 + lo1 + up2 + lo2 + up3 + lo3 - 6.0 * mid[c]
            advect = 0.5 * (mid[0] * (up1 - lo1) + mid[1] * (up2 - lo2) + mid[2] * (up3 - lo3))
            new.append(mid[c] + time_step * (nu * laplace - advect))
        store(x, new)
        return carry
    lax.fori_loop(start, stop, body, 0)

def split3(x):
    high = x.astype(jnp.bfloat16); rest = x - high.astype(jnp.float32)
    mid = rest.astype(jnp.bfloat16)
    low = (rest - mid.astype(jnp.float32)).astype(jnp.bfloat16)
    return high, mid, low

def permuted(onehot, x):
    n = x.shape[1]
    parts = jnp.dot(onehot, jnp.concatenate(split3(x), axis=1), preferred_element_type=jnp.float32)
    return parts[:, :n] + parts[:, n:2 * n] + parts[:, 2 * n:]

def swap_groups(x):
    row = lax.broadcasted_iota(jnp.int32, x.shape, 0)
    lane = lax.broadcasted_iota(jnp.int32, x.shape, 1)
    for b in range(4):
        k = 1 << b
        rb, lb = (row >> b) & 1, (lane >> (3 + b)) & 1
        above = pltpu.roll(pltpu.roll(x, 256 - k, 0), 8 * k, 1)
        below = pltpu.roll(pltpu.roll(x, k, 0), 128 - 8 * k, 1)
        x = jnp.where(rb == lb, x, jnp.where(rb == 0, above, below))
    return x

def send_order(assign, sample):
    target = assign // 256
    column = jnp.transpose(jnp.broadcast_to(target, (128, 256)))[:, :1]
    before = lax.broadcasted_iota(jnp.int32, (256, 256), 0) < lax.broadcasted_iota(jnp.int32, (256, 256), 1)
    same = jnp.where((column == target) & before, 1, 0)
    rank = jnp.sum(same, axis=0, keepdims=True)
    dst = lax.broadcasted_iota(jnp.int32, (128, 256), 0)
    rows = [jnp.where((target == dst) & (rank == j), 1.0, 0.0) for j in range(2)]
    chosen = jnp.concatenate(rows, axis=0).astype(jnp.bfloat16)
    patch = jnp.where(sample == lax.broadcasted_iota(jnp.int32, (256, 256), 0), 1.0, 0.0).astype(jnp.bfloat16)
    return lax.dot_general(chosen, patch, (((1,), (1,)), ((), ())), preferred_element_type=jnp.float32).astype(jnp.bfloat16)

GATHER = ((0, 72), (72, 80), (152, 80))

def front_kernel(params, vel, visc, assign, sample, nxt, out, got, ext, vext, first, order, slots, s0, *rest):
    s1, s2, s3, relay = rest[0:3], rest[3:6], rest[6:9], rest[9:27]
    hs, hr, lsem, ssem, rsem, cs, cr, xs, xr, xl = rest[27:]
    xyz, core = coords()
    me = lax.axis_index("group") * 32 + lax.axis_index("dev")
    after, before = (me + 1) % 128, (me + 127) % 128
    after_id, before_id = (after // 32, after % 32), (before // 32, before % 32)
    block = (xyz[2] // 2, core, xyz[2] % 2, xyz[1], xyz[0])
    number = assign[...].astype(jnp.float32)
    slots[...] = jnp.zeros((8, 128), jnp.float32)
    slots[0:1] = number[:, :128]
    slots[1:2] = number[:, 128:]
    own = [pltpu.make_async_copy(params, out.at[block + (pl.ds(0, 224),)], lsem.at[0]),
           pltpu.make_async_copy(slots, out.at[block + (pl.ds(224, 8),)], lsem.at[1])]
    for c in own: c.start()
    barrier = pltpu.get_barrier_semaphore()
    ids = neighbours(xyz, core) + [ident(shifted(xyz, a, 2), core) for a in range(3)] + [after_id, before_id]
    for i in ids:
        pl.semaphore_signal(barrier, inc=1, device_id=i, device_id_type=MESH)
    ext[:, 2:10] = vel[...]
    vext[1:9] = visc[...]
    pl.semaphore_wait(barrier, len(ids))
    sib = ident(xyz, 1 - core)
    pend = []

    def remote(src, dst, s, r, to):
        c = pltpu.make_async_remote_copy(src_ref=src, dst_ref=dst, send_sem=s, recv_sem=r, device_id=to, device_id_type=MESH)
        c.start(); pend.append(c)
        return c

    sibs = []
    def to_sib(src):
        k = len(sibs)
        sibs.append(remote(src, src, cs.at[k], cr.at[k], sib))
    steps = {}
    def around(p, phase):
        a = ORDERS[p][phase]; full = ORDERS[p][:phase]
        at = [shifted(xyz, a, k) for k in range(4)]
        return full, at, ident(at[1], core), ident(at[3], core), halves(p, GATHER), (phase * 3 + p) * 6, GATHER[p]
    def g_send(p, phase, kind, at, half, to):
        full, _, _, _, hs_, base, _ = around(p, phase)
        r0, n = hs_[half]
        src = region(out, full, at, core, r0, n)
        steps[p, phase, kind] = remote(src, src, ssem.at[base + kind], rsem.at[base + kind], to)
    def g_start(phase):
        for p in range(3):
            full, at, R, L, hv, base, (r0, n) = around(p, phase)
            if phase == 0:
                src = region(out, full, at[0], core, r0, n)
                for kind, k in ((2, 2), (0, 1), (3, 3)):
                    steps[p, 0, kind] = remote(src, src, ssem.at[base + kind], rsem.at[base + kind], ident(at[k], core))
                continue
            g_send(p, phase, 0, at[0], 0, R)
            g_send(p, phase, 3, at[0], 1, L)
            g_send(p, phase, 1, at[0], 1, R)
            g_send(p, phase, 4, at[0], 0, L)
            if phase == 2: to_sib(region(out, full, at[0], core, r0, n))
    def g_forward(phase):
        for p in range(3):
            full, at, R, L, hv, base, _ = around(p, phase)
            steps[p, phase, 0].wait_recv(); g_send(p, phase, 2, at[3], 0, R)
            steps[p, phase, 3].wait_recv(); g_send(p, phase, 5, at[1], 1, L)
    def g_near(phase):
        for p in range(3):
            full, at, R, L, hv, base, (r0, n) = around(p, phase)
            steps[p, phase, 1].wait_recv(); steps[p, phase, 4].wait_recv()
            if phase == 2:
                to_sib(region(out, full, at[3], core, r0, n))
                to_sib(region(out, full, at[1], core, r0, n))
    def g_far(phase):
        for p in range(3):
            full, at, R, L, hv, base, (r0, n) = around(p, phase)
            steps[p, phase, 2].wait_recv(); steps[p, phase, 5].wait_recv()
            if phase == 2: to_sib(region(out, full, at[2], core, r0, n))

    moves, selfs = {}, {}
    def x_core():
        blocks = s0.reshape(2, 2, 2, 4, 4, 48, 128)
        for p in range(3):
            for zh in range(2):
                k = p * 2 + zh
                rows = pl.ds(16 * p, 16)
                moves[p, 0, zh] = remote(blocks.at[zh, 1 - core, :, :, :, rows], s1[p].at[core, zh], xs.at[k], xr.at[k], sib)
                selfs[p, 0, zh] = pltpu.make_async_copy(blocks.at[zh, core, :, :, :, rows], s1[p].at[core, zh], xl.at[k])
                selfs[p, 0, zh].start()
    def stage(p, s):
        a = ORDERS[p][s - 1]; others = ORDERS[p][s:]
        src = (s1, s2, s3)[s - 1][p]
        dst = got.at[p] if s == 3 else (s2, s3)[s - 1][p]
        at = [shifted(xyz, a, k) for k in range(4)]
        left = (slice(None),) * s
        def part(k, r0, n): return src.at[left + pick(others, at[k], (a,) + others) + (pl.ds(r0, n),)]
        free = (slice(None),) * (s + len(dims(others)))
        def land(k, r0, n): return dst.at[(at[k][a],) + free + (pl.ds(r0, n),)]
        return part, land, ident(at[1], core), ident(at[3], core), 6 + ((s - 1) * 3 + p) * 6
    def x_start(s):
        for p in range(3):
            part, land, R, L, base = stage(p, s)
            if s == 1:
                for zh in range(2): moves[p, 0, zh].wait_recv(); selfs[p, 0, zh].wait()
            else:
                for k in (0, 1, 4, 5): moves[p, s - 1, k].wait_recv()
                selfs[p, s - 1].wait()
            def mv(k, src, dst, to): moves[p, s, k] = remote(src, dst, xs.at[base + k], xr.at[base + k], to)
            via = relay[((s - 1) * 3 + p) * 2], relay[((s - 1) * 3 + p) * 2 + 1]
            mv(2, part(2, 0, 8), via[0], R)
            mv(3, part(2, 8, 8), via[1], L)
            mv(0, part(1, 0, 16), land(0, 0, 16), R)
            mv(1, part(3, 0, 16), land(0, 0, 16), L)
            c = pltpu.make_async_copy(part(0, 0, 16), land(0, 0, 16), xl.at[6 + (s - 1) * 3 + p])
            c.start(); selfs[p, s] = c
    def x_relay(s):
        for p in range(3):
            part, land, R, L, base = stage(p, s)
            via = relay[((s - 1) * 3 + p) * 2], relay[((s - 1) * 3 + p) * 2 + 1]
            moves[p, s, 2].wait_recv()
            moves[p, s, 4] = remote(via[0], land(3, 0, 8), xs.at[base + 4], xr.at[base + 4], R)
            moves[p, s, 3].wait_recv()
            moves[p, s, 5] = remote(via[1], land(1, 8, 8), xs.at[base + 5], xr.at[base + 5], L)
    def x_finish():
        for p in range(3):
            for k in (0, 1, 4, 5): moves[p, 3, k].wait_recv()
            selfs[p, 3].wait()

    def put_first(x, new):
        for c in range(3): first[c, x] = new[c]
    def put_next(x, new):
        for c in range(3): nxt[c, x] = new[c]
    for c in own: c.wait()
    g_start(0)
    halo = [remote(vel.at[:, 6:8], ext.at[:, 0:2], hs.at[0], hr.at[0], after_id),
            remote(vel.at[:, 0:2], ext.at[:, 10:12], hs.at[1], hr.at[1], before_id),
            remote(visc.at[7:8], vext.at[0:1], hs.at[2], hr.at[2], after_id),
            remote(visc.at[0:1], vext.at[9:10], hs.at[3], hr.at[3], before_id)]
    order[...] = send_order(assign[...], sample[...])
    advance_planes(ext, vext, 2, 8, put_first)
    for p in range(3):
        for kind in (0, 2, 3): steps[p, 0, kind].wait_recv()
    g_start(1)
    for c in halo: c.wait_recv()
    lower = jnp.where(me > 0, 1.0, 0.0); upper = jnp.where(me < 127, 1.0, 0.0)
    ext[:, 0:2] = ext[:, 0:2] * lower
    vext[0:1] = vext[0:1] * lower
    ext[:, 10:12] = ext[:, 10:12] * upper
    vext[9:10] = vext[9:10] * upper
    advance_planes(ext, vext, 0, 2, put_first)
    advance_planes(ext, vext, 8, 10, put_first)
    g_forward(1)
    advance_planes(first, visc, 0, 8, put_next)
    g_near(1); g_far(1)
    g_start(2)
    def body(i, carry):
        c, q = i // 4, i % 4
        for field, ref, off in ((0, first, 1), (1, nxt, 0)):
            a, b = ref[c, 2 * q + off], ref[c, 2 * q + off + 1]
            pieces = []
            for iy in range(16):
                pieces += [a[iy * 8:iy * 8 + 8], b[iy * 8:iy * 8 + 8]]
            res = permuted(order[...], swap_groups(jnp.concatenate(pieces, axis=0)))
            for j in range(2):
                s0[pl.ds(j * 24 + field * 12 + i, 128, stride=48), :] = res[j * 128:(j + 1) * 128]
        return carry
    lax.fori_loop(0, 12, body, 0)
    x_core()
    g_forward(2)
    x_start(1)
    g_near(2)
    x_relay(1)
    x_start(2)
    g_far(2)
    x_relay(2)
    x_start(3)
    x_relay(3)
    x_finish()
    for c in sibs: c.wait_recv()
    for c in pend: c.wait_send()

def front(params, vel, visc, assign, sample):
    f32, V = jnp.float32, pltpu.VMEM
    scratch = [V((3, 12, 128, 128), f32), V((10, 128, 128), f32), V((3, 10, 128, 128), f32), V((256, 256), jnp.bfloat16), V((8, 128), f32), V((6144, 128), f32)]
    scratch += [V((2, 2, 2, 4, 4, 16, 128), f32)] * 3
    for s in (2, 3):
        for p in range(3):
            scratch.append(V((4,) * (s - 1) + (2,) + dims(ORDERS[p][s - 1:]) + (16, 128), f32))
    for s in (1, 2, 3):
        for p in range(3):
            scratch += [V((4,) * (s - 1) + (2,) + dims(ORDERS[p][s:]) + (8, 128), f32)] * 2
    D = pltpu.SemaphoreType.DMA
    scratch += [D((4,)), D((4,)), D((2,)), D((54,)), D((54,)), D((12,)), D((12,)), D((60,)), D((60,)), D((15,))]
    A = pl.BlockSpec(memory_space=pl.ANY); M = pl.BlockSpec(memory_space=pltpu.VMEM)
    return pl.pallas_call(
        front_kernel,
        out_shape=(jax.ShapeDtypeStruct((3, 8, 128, 128), f32), jax.ShapeDtypeStruct((2, 2, 2, 4, 4, 232, 128), f32),
                   jax.ShapeDtypeStruct((3, 4, 4, 4, 2, 16, 128), f32)),
        in_specs=[A, M, M, M, M], out_specs=(M, A, A), scratch_shapes=scratch,
        compiler_params=pltpu.CompilerParams(collective_id=0, has_side_effects=True, vmem_limit_bytes=58 << 20),
        name="front",
    )(params, vel, visc, assign, sample)

BLOCK = 232
WIN, WUP, WDN, WOUT = (0, 1536, 4), (6144, 512, 16), (14336, 2048, 4), (22528, 512, 12)
NN = (((1,), (0,)), ((), ())); NT = (((1,), (1,)), ((), ()))

def split2(x):
    high = x.astype(jnp.bfloat16)
    return high, (x - high.astype(jnp.float32)).astype(jnp.bfloat16)

def dot3(a, b, form):
    d = lambda p, q: lax.dot_general(p, q, form, preferred_element_type=jnp.float32)
    return d(a[0], b[0]) + (d(a[0], b[1]) + d(a[1], b[0]))

def put2(refs, value, *at):
    for r, v in zip(refs, split2(value)): r[at] = v

def unpack(flat, spec, hi, lo):
    base, rows, cols = spec
    n = 256
    def body(i, carry):
        for q in range(cols):
            start = base + i * (n * cols) + q
            h, l = split2(flat[pl.ds(start, n, stride=cols), :])
            at = (pl.ds(pl.multiple_of(i * n, n), n), pl.ds(q * 128, 128))
            hi[at] = h; lo[at] = l
        return carry
    lax.fori_loop(0, rows // n, body, 0)

def pack(flat, spec, r0, n, c0, value):
    base, rows, cols = spec
    for q in range(value.shape[1] // 128):
        flat[pl.ds(base + r0 * cols + c0 + q, n, stride=cols), :] = value[:, q * 128:(q + 1) * 128]

def slot_matrices(assign, me):
    mine = (assign // 256) == me
    t = lax.broadcasted_iota(jnp.int32, (128, 256), 1)
    first = jnp.min(jnp.where(mine, t, 512), axis=1, keepdims=True)
    last = jnp.max(jnp.where(mine, t, -1), axis=1, keepdims=True)
    slot = assign % 256
    cols = [jnp.sum(jnp.where(t == at, slot, 0), axis=1, keepdims=True) for at in (first, last)]
    want = [jnp.where(c == t, 1.0, 0.0).astype(jnp.bfloat16) for c in cols]
    k = lax.broadcasted_iota(jnp.int32, (128, 128), 0)
    src = lax.broadcasted_iota(jnp.int32, (128, 128), 1)
    moved = []
    for p in range(3):
        co = {ORDERS[p][2]: k // 32, ORDERS[p][1]: (k // 8) % 4, ORDERS[p][0]: (k // 2) % 4}
        flat = (co[2] // 2) * 64 + (k % 2) * 32 + (co[2] % 2) * 16 + co[1] * 4 + co[0]
        perm = jnp.where(flat == src, 1.0, 0.0).astype(jnp.bfloat16)
        moved.append([jnp.dot(perm, w, preferred_element_type=jnp.float32) for w in want])
    return [jnp.transpose(jnp.concatenate([moved[p0][0], moved[p1][1]], axis=0)).astype(jnp.bfloat16) for p0, p1 in PAIRS]

PAIRS = ((0, 1), (0, 2), (1, 2))

def back_kernel(got, gathered, pred, mine, flat, asg, win, winl, wup, wupl, wdn, wdnl, wout, woutl,
                 x, tgt, xs, xsl, hid, pre, a5, a5l, state, state2, rowsc, crecv, *rest):
    bufs, (sem, cs, cr, ssem, rsem) = rest[:33], rest[33:]
    me = lax.axis_index("group") * 32 + lax.axis_index("dev")
    xyz, core = coords()
    barrier = pltpu.get_barrier_semaphore()
    ids = neighbours(xyz, core) + [ident(shifted(xyz, a, 2), core) for a in range(3)]
    for i in ids:
        pl.semaphore_signal(barrier, inc=1, device_id=i, device_id_type=MESH)
    ac = pltpu.make_async_copy(gathered.at[:, pl.ds(224, 8), :], asg, sem.at[0])
    wc = pltpu.make_async_copy(gathered.at[:, pl.ds(0, 224), :], flat.reshape(128, 224, 128), sem.at[1])
    ac.start(); wc.start()
    ac.wait()
    assign = jnp.concatenate([asg[:, 0, :], asg[:, 1, :]], axis=1).astype(jnp.int32)
    for i, place in enumerate(slot_matrices(assign, me)): rowsc[i] = place
    for field, ref in ((0, x), (1, tgt)):
        for k in range(12):
            col = [j * 24 + field * 12 + k for j in range(2)]
            src = jnp.concatenate([got[pl.ds((c // 16) * 2048 + c % 16, 128, stride=16), :] for c in col], axis=0)
            ref[:, k * 128:(k + 1) * 128] = permuted(rowsc[(col[0]) // 8], src)
    wc.wait()
    unpack(flat, WIN, win, winl)
    unpack(flat, WUP, wup, wupl)
    unpack(flat, WDN, wdn, wdnl)
    unpack(flat, WOUT, wout, woutl)
    put2((xs, xsl), x[...], slice(None), slice(None))
    state[...] = dot3((xs[...], xsl[...]), (win[...], winl[...]), NN)
    s = state[...]
    r = lax.rsqrt(jnp.mean(s * s, axis=1, keepdims=True) + norm_epsilon)
    put2((a5, a5l), s * r, slice(None), slice(None))
    c1, c2 = 0.7978845608028654, 0.044715
    def up(n, carry):
        at = (slice(None), pl.ds(pl.multiple_of(n * 1024, 1024), 1024))
        p = dot3((a5[...], a5l[...]), (wup[at], wupl[at]), NN)
        th = jnp.tanh(c1 * (p + c2 * (p * p * p)))
        pre[at] = 0.5 * (1.0 + th) + 0.5 * p * (1.0 - th * th) * (c1 * (1.0 + (3.0 * c2) * (p * p)))
        hid[at] = 0.5 * p * (1.0 + th)
        return carry
    lax.fori_loop(0, 2, up, 0)
    def down(n, acc):
        at = (slice(None), pl.ds(pl.multiple_of(n * 1024, 1024), 1024))
        wat = (pl.ds(pl.multiple_of(n * 1024, 1024), 1024), slice(None))
        return acc + dot3(split2(hid[at]), (wdn[wat], wdnl[wat]), NN)
    state2[...] = lax.fori_loop(0, 2, down, s)
    s2 = split2(state2[...])
    def outp(n, carry):
        at = (slice(None), pl.ds(pl.multiple_of(n * 768, 768), 768))
        g = x[at] + dot3(s2, (wout[at], woutl[at]), NN)
        pred[at] = g
        tgt[at] = (g - tgt[at]) * (1.0 / 256.0)
        return carry
    lax.fori_loop(0, 2, outp, 0)
    blocks = flat.reshape(2, 2, 2, 4, 4, 224, 128)
    sib = ident(xyz, 1 - core)
    def swap(n):
        src, dst = (blocks.at[1, 1 - core], crecv.at[1]) if n == 0 else (blocks.at[0, 1 - core, n - 1], crecv.at[0, n - 1])
        return pltpu.make_async_remote_copy(src_ref=src, dst_ref=dst, send_sem=cs.at[n], recv_sem=cr.at[n], device_id=sib, device_id_type=MESH)
    def swap_add(n):
        swap(n).wait_recv()
        def body(i, carry):
            at = ((1, i // 16) if n == 0 else (0, n - 1)) + ((i // 4) % 4, i % 4)
            mineat = (at[0], core) + at[1:]
            blocks[mineat] = blocks[mineat] + crecv[at]
            return carry
        lax.fori_loop(0, 32 if n == 0 else 16, body, 0)
    s2t = split2(jnp.transpose(state2[...]))
    def gout(n, acc):
        at = (slice(None), pl.ds(pl.multiple_of(n * 768, 768), 768))
        e = split2(tgt[at])
        pack(flat, WOUT, 0, 512, n * 6, dot3(s2t, e, NN))
        return acc + dot3(e, (wout[at], woutl[at]), NT)
    ds2 = lax.fori_loop(0, 2, gout, jnp.zeros((256, 512), jnp.float32))
    state2[...] = ds2
    put2((xs, xsl), ds2, slice(None), pl.ds(0, 512))
    dss = lambda: (xs[:, :512], xsl[:, :512])
    normt = jnp.transpose(state[...] * r)
    nt = split2(normt)
    def gdown(n, carry):
        at = (slice(None), pl.ds(pl.multiple_of(n * 1024, 1024), 1024))
        pack(flat, WDN, n * 1024, 1024, 0, dot3(split2(jnp.transpose(hid[at])), dss(), NN))
        return carry
    lax.fori_loop(0, 2, gdown, 0)
    pl.semaphore_wait(barrier, len(ids))
    swap(0).start()
    def hidden(n, acc):
        at = (slice(None), pl.ds(pl.multiple_of(n * 512, 512), 512))
        wat = (pl.ds(pl.multiple_of(n * 512, 512), 512), slice(None))
        dh = dot3(dss(), (wdn[wat], wdnl[wat]), NT)
        dps = split2(dh * pre[at])
        pack(flat, WUP, 0, 512, n * 4, dot3(nt, dps, NN))
        return acc + dot3(dps, (wup[at], wupl[at]), NT)
    pend = []
    first, second, third = big_phase(blocks, bufs, ssem, rsem, xyz, core, pend)
    lower, upper = (0, 1, 2), (3, 4)
    dn = lax.fori_loop(0, 2, hidden, jnp.zeros((256, 512), jnp.float32))
    swap_add(0)
    first(upper)
    dn = lax.fori_loop(2, 4, hidden, dn)
    @pl.when(core == 0)
    def _():
        swap(1).start()
        swap(2).start()
    second(upper)
    norm = state[...] * r
    ds = state2[...] + r * (dn - norm * jnp.mean(dn * norm, axis=1, keepdims=True))
    put2((a5, a5l), ds, slice(None), slice(None))
    def gin(n, carry):
        at = (slice(None), pl.ds(pl.multiple_of(n * 512, 512), 512))
        pack(flat, WIN, n * 512, 512, 0, dot3(split2(jnp.transpose(x[at])), (a5[...], a5l[...]), NN))
        return carry
    lax.fori_loop(0, 2, gin, 0)
    @pl.when(core == 1)
    def _(): swap(1).start()
    lax.fori_loop(2, 3, gin, 0)
    @pl.when(core == 1)
    def _(): swap(2).start()
    swap_add(1)
    swap_add(2)
    first(lower)
    third(upper)
    second(lower)
    third(lower)
    small_phases(blocks, mine, bufs[12:], ssem, rsem, xyz, core, pend)
    for c in pend: c.wait_send()
    for n in range(3): swap(n).wait_send()

SPREAD = ((0, 48), (48, 88), (136, 88))
UNITS = ((0, None), (1, 0), (2, 0), (1, 1), (2, 1))

def place(full, at, core, r0, n, half=None):
    i = pick(full, at)
    if half is not None: i = (half,) + i[1:]
    return (i[0], core) + i[1:] + (pl.ds(r0, n), slice(None))

def walk_half(full, xyz, half, body):
    sizes = [2 if a == 2 and half is not None else 4 for a in full]
    count = 1
    for n in sizes: count *= n
    def step(i, carry):
        at = list(xyz)
        for a, n in zip(full, sizes):
            at[a] = i % n + (2 * half if n == 2 else 0)
            i = i // n
        body(tuple(at)); return carry
    lax.fori_loop(0, count, step, 0)

def big_phase(blocks, bufs, ssem, rsem, xyz, core, pend):
    copies = {}
    def of(u):
        p, half = UNITS[u]; a = ORDERS[p][2]; full = ORDERS[p][:2]
        ids = [ident(shifted(xyz, a, k), core) for k in range(4)]
        refs = [b if half is None else b.at[half] for b in bufs[p * 4:p * 4 + 4]]
        lead = (slice(None),) * (len(dims(full)) - (half is not None))
        return p, half, a, full, ids, refs, lead
    def send(u, kind, rel, r0, n, to, dst):
        p, half, a, full, ids, _, _ = of(u)
        c = pltpu.make_async_remote_copy(src_ref=blocks.at[place(full, shifted(xyz, a, rel), core, r0, n, half)], dst_ref=dst,
            send_sem=ssem.at[u * 6 + kind], recv_sem=rsem.at[u * 6 + kind], device_id=ids[to], device_id_type=MESH)
        c.start(); copies[u, kind] = c; pend.append(c)
    def fold(u, kind, rel, r0, n, slot, off):
        p, half, a, full, _, _, _ = of(u)
        copies[u, kind].wait_recv()
        ref = bufs[p * 4 + slot]
        def body(at):
            i = place((), at, core, r0, n)
            blocks[i] = blocks[i] + ref[pick((), at, full) + (pl.ds(off, n), slice(None))]
        walk_half(full, shifted(xyz, a, rel), half, body)
    def first(units):
        for u in units:
            p, _, _, _, _, refs, lead = of(u)
            (h0, n0), (h1, n1) = halves(p, SPREAD)
            send(u, 0, 2, h0, n0, 1, refs[0])
            send(u, 3, 2, h1, n1, 3, refs[1])
        for u in units:
            p, _, _, _, _, refs, lead = of(u)
            (h0, n0), (h1, n1) = halves(p, SPREAD)
            send(u, 1, 1, h1, n1, 1, refs[2].at[lead + (pl.ds(n0, n1),)])
            send(u, 4, 3, h0, n0, 3, refs[3].at[lead + (pl.ds(0, n0),)])
    def second(units):
        for u in units:
            p, _, _, _, _, refs, lead = of(u)
            (h0, n0), (h1, n1) = halves(p, SPREAD)
            fold(u, 0, 1, h0, n0, 0, 0); send(u, 2, 1, h0, n0, 1, refs[2].at[lead + (pl.ds(0, n0),)])
            fold(u, 3, 3, h1, n1, 1, 0); send(u, 5, 3, h1, n1, 3, refs[3].at[lead + (pl.ds(n0, n1),)])
    def third(units):
        for u in units:
            (h0, n0), (h1, n1) = halves(UNITS[u][0], SPREAD)
            fold(u, 1, 0, h1, n1, 2, n0); fold(u, 4, 0, h0, n0, 3, 0)
        for u in units:
            (h0, n0), (h1, n1) = halves(UNITS[u][0], SPREAD)
            fold(u, 2, 0, h0, n0, 2, 0); fold(u, 5, 0, h1, n1, 3, n0)
    return first, second, third

def small_phases(blocks, mine, bufs, ssem, rsem, xyz, core, pend):
    copies = {}
    def send(p, phase, kind, rel, r0, n, to, dst):
        a = ORDERS[p][2 - phase]; full = ORDERS[p][:2 - phase]
        k = 30 + ((phase - 1) * 3 + p) * 6 + kind
        c = pltpu.make_async_remote_copy(src_ref=blocks.at[place(full, shifted(xyz, a, rel), core, r0, n)], dst_ref=dst,
            send_sem=ssem.at[k], recv_sem=rsem.at[k], device_id=ident(shifted(xyz, a, to), core), device_id_type=MESH)
        c.start(); copies[p, phase, kind] = c; pend.append(c)
    def fold(p, phase, kind, rel, r0, n, ref, off):
        a = ORDERS[p][2 - phase]; full = ORDERS[p][:2 - phase]
        copies[p, phase, kind].wait_recv()
        def body(at):
            i = place((), at, core, r0, n)
            blocks[i] = blocks[i] + ref[pick((), at, full) + (pl.ds(off, n), slice(None))]
        walk(full, shifted(xyz, a, rel), body)
    for p in range(3):
        b = bufs[p * 4:p * 4 + 4]; (h0, n0), (h1, n1) = halves(p, SPREAD)
        lead = (slice(None),) * len(dims(ORDERS[p][:1]))
        send(p, 1, 0, 2, h0, n0, 1, b[0])
        send(p, 1, 3, 2, h1, n1, 3, b[1])
        send(p, 1, 1, 1, h1, n1, 1, b[2].at[lead + (pl.ds(n0, n1),)])
        send(p, 1, 4, 3, h0, n0, 3, b[3].at[lead + (pl.ds(0, n0),)])
    for p in range(3):
        b = bufs[p * 4:p * 4 + 4]; (h0, n0), (h1, n1) = halves(p, SPREAD)
        lead = (slice(None),) * len(dims(ORDERS[p][:1]))
        fold(p, 1, 0, 1, h0, n0, b[0], 0); send(p, 1, 2, 1, h0, n0, 1, b[2].at[lead + (pl.ds(0, n0),)])
        fold(p, 1, 3, 3, h1, n1, b[1], 0); send(p, 1, 5, 3, h1, n1, 3, b[3].at[lead + (pl.ds(n0, n1),)])
    for p in range(3):
        b = bufs[p * 4:p * 4 + 4]; (h0, n0), (h1, n1) = halves(p, SPREAD)
        fold(p, 1, 1, 0, h1, n1, b[2], n0); fold(p, 1, 4, 0, h0, n0, b[3], 0)
    for p in range(3):
        b = bufs[p * 4:p * 4 + 4]; (h0, n0), (h1, n1) = halves(p, SPREAD)
        fold(p, 1, 2, 0, h0, n0, b[2], 0); fold(p, 1, 5, 0, h1, n1, b[3], n0)
        b = bufs[12 + p * 3:15 + p * 3]; r0, n = SPREAD[p]
        send(p, 2, 0, 2, r0, n, 2, b[2])
        send(p, 2, 1, 1, r0, n, 1, b[0])
        send(p, 2, 2, 3, r0, n, 3, b[1])
    for p in range(3):
        b = bufs[12 + p * 3:15 + p * 3]; r0, n = SPREAD[p]
        fold(p, 2, 0, 0, r0, n, b[2], 0); fold(p, 2, 1, 0, r0, n, b[0], 0); fold(p, 2, 2, 0, r0, n, b[1], 0)
    mine[...] = blocks[(xyz[2] // 2, core, xyz[2] % 2, xyz[1], xyz[0])]

def back(got, gathered):
    f32, b16 = jnp.float32, jnp.bfloat16
    V = pltpu.VMEM
    both = lambda *s: [V(s, b16), V(s, b16)]
    slots = []
    for phase in range(2):
        for p in range(3):
            lead = dims(ORDERS[p][:2 - phase]); (_, n0), (_, n1) = halves(p, SPREAD)
            slots += [V(lead + (n, 128), f32) for n in (n0, n1, n0 + n1, n0 + n1)]
    for p in range(3): slots += [V((SPREAD[p][1], 128), f32)] * 3
    return pl.pallas_call(
        back_kernel,
        out_shape=(jax.ShapeDtypeStruct((256, 1536), f32), jax.ShapeDtypeStruct((224, 128), f32)),
        in_specs=[pl.BlockSpec(memory_space=pltpu.VMEM), pl.BlockSpec(memory_space=pl.ANY)],
        out_specs=(pl.BlockSpec(memory_space=pltpu.VMEM), pl.BlockSpec(memory_space=pltpu.VMEM)),
        scratch_shapes=[V((28672, 128), f32), V((128, 8, 128), f32)] + both(1536, 512) + both(512, 2048) + both(2048, 512) + both(512, 1536)
            + [V((256, 1536), f32), V((256, 1536), f32)] + both(256, 1536) + [V((256, 2048), f32), V((256, 2048), f32)] + both(256, 512)
            + [V((256, 512), f32), V((256, 512), f32), V((3, 256, 256), b16), V((2, 2, 4, 4, 224, 128), f32)] + slots
            + [pltpu.SemaphoreType.DMA((n,)) for n in (2, 3, 3, 66, 66)],
        compiler_params=pltpu.CompilerParams(collective_id=1, has_side_effects=True, vmem_limit_bytes=61 << 20),
        name="back",
    )(got, gathered)

def adam(shard, grad, moment, second):
    new_m = beta_first * moment + (1.0 - beta_first) * grad
    new_v = beta_second * second + (1.0 - beta_second) * grad * grad
    update = (
        new_m
        / (1.0 - beta_first**adam_count)
        / (jnp.sqrt(new_v / (1.0 - beta_second**adam_count)) + adam_epsilon)
    )
    return (shard - learn_rate * update, new_m, new_v)

def local(velocity, viscosity, sample_idx, assign, params, adam_m, adam_v):
    velocity_next, gathered, got = front(params.reshape(224, 128), velocity, viscosity, assign, sample_idx)
    prediction, grad = back(got.reshape(6144, 128), gathered.reshape(128, 232, 128))
    new_params, new_m, new_v = adam(params, grad.reshape(-1), adam_m, adam_v)
    return (velocity_next, prediction, new_params, new_m, new_v)


def solution(mesh):
    placed = (
        P(None, ("group", "dev"), None, None),
        P(("group", "dev"), None, None),
        P(("group", "dev"), None),
        P(("group", "dev"), None),
        P(("group", "dev")),
        P(("group", "dev")),
        P(("group", "dev")),
    )
    return jax.shard_map(
        local,
        mesh=mesh,
        in_specs=placed,
        out_specs=(
            P(None, ("group", "dev"), None, None),
            P(("group", "dev"), None),
            P(("group", "dev")),
            P(("group", "dev")),
            P(("group", "dev")),
        ),
        check_vma=False,
    )
```

```python
import jax
import jax.numpy as jnp
from jax import lax
from jax.experimental import pallas as pl
from jax.experimental.pallas import tpu as pltpu
from jax.sharding import PartitionSpec as P

time_step = 0.5
norm_epsilon = 1e-06
beta_first = 0.9
beta_second = 0.95
learn_rate = 0.01
adam_epsilon = 1e-08
adam_count = 10

MESH = pl.DeviceIdType.MESH
PIECES = ((0, 72), (72, 80), (152, 72))
ORDERS = ((0, 1, 2), (1, 2, 0), (2, 0, 1))

def coords():
    g = lax.axis_index("group"); d = lax.axis_index("dev")
    return (d % 4, (d // 4) % 4, (g // 2) * 2 + d // 16), g % 2

def ident(xyz, core):
    x, y, z = xyz
    return ((z // 2) * 2 + core, (z % 2) * 16 + y * 4 + x)

def shifted(xyz, axis, by):
    out = list(xyz); out[axis] = (xyz[axis] + by) % 4
    return tuple(out)

def neighbours(xyz, core):
    ids = [ident(shifted(xyz, a, s), core) for a in range(3) for s in (1, 3)]
    return ids + [ident(xyz, 1 - core)]

def region(ref, full, xyz, core, r0, n):
    x = slice(None) if 0 in full else xyz[0]
    y = slice(None) if 1 in full else xyz[1]
    zh = slice(None) if 2 in full else xyz[2] // 2
    zl = slice(None) if 2 in full else xyz[2] % 2
    return ref.at[zh, core, zl, y, x, pl.ds(r0, n), :]

def halves(piece, pieces=PIECES):
    r0, n = pieces[piece]
    n0 = (n // 16) * 8 if n % 16 else n // 2
    return (r0, n0), (r0 + n0, n - n0)


def pick(full, xyz, present=(0, 1, 2)):
    out = []
    if 2 in present: out += [slice(None)] * 2 if 2 in full else [xyz[2] // 2, xyz[2] % 2]
    if 1 in present: out += [slice(None)] if 1 in full else [xyz[1]]
    if 0 in present: out += [slice(None)] if 0 in full else [xyz[0]]
    return tuple(out)

def walk(full, xyz, body):
    full = tuple(full)
    if not full:
        body(xyz); return
    def step(i, carry):
        at = list(xyz)
        for k, a in enumerate(full):
            at[a] = (i // (4 ** k)) % 4
        body(tuple(at)); return carry
    lax.fori_loop(0, 4 ** len(full), step, 0)

def dims(present):
    out = ()
    if 2 in present: out += (2, 2)
    if 1 in present: out += (4,)
    if 0 in present: out += (4,)
    return out


def advance_planes(ext, visc, start, stop, store):
    def body(x, carry):
        mid = [ext[c, x + 1] for c in range(3)]
        nu = visc[x]
        new = []
        for c in range(3):
            up1, lo1 = ext[c, x + 2], ext[c, x]
            up2, lo2 = pltpu.roll(mid[c], 127, 0), pltpu.roll(mid[c], 1, 0)
            up3, lo3 = pltpu.roll(mid[c], 127, 1), pltpu.roll(mid[c], 1, 1)
            laplace = up1 + lo1 + up2 + lo2 + up3 + lo3 - 6.0 * mid[c]
            advect = 0.5 * (mid[0] * (up1 - lo1) + mid[1] * (up2 - lo2) + mid[2] * (up3 - lo3))
            new.append(mid[c] + time_step * (nu * laplace - advect))
        store(x, new)
        return carry
    lax.fori_loop(start, stop, body, 0)

def split3(x):
    high = x.astype(jnp.bfloat16); rest = x - high.astype(jnp.float32)
    mid = rest.astype(jnp.bfloat16)
    low = (rest - mid.astype(jnp.float32)).astype(jnp.bfloat16)
    return high, mid, low

def permuted(onehot, x):
    n = x.shape[1]
    parts = jnp.dot(onehot, jnp.concatenate(split3(x), axis=1), preferred_element_type=jnp.float32)
    return parts[:, :n] + parts[:, n:2 * n] + parts[:, 2 * n:]

def swap_groups(x):
    row = lax.broadcasted_iota(jnp.int32, x.shape, 0)
    lane = lax.broadcasted_iota(jnp.int32, x.shape, 1)
    for b in range(4):
        k = 1 << b
        rb, lb = (row >> b) & 1, (lane >> (3 + b)) & 1
        above = pltpu.roll(pltpu.roll(x, 256 - k, 0), 8 * k, 1)
        below = pltpu.roll(pltpu.roll(x, k, 0), 128 - 8 * k, 1)
        x = jnp.where(rb == lb, x, jnp.where(rb == 0, above, below))
    return x

def send_order(assign, sample):
    target = assign // 256
    column = jnp.transpose(jnp.broadcast_to(target, (128, 256)))[:, :1]
    before = lax.broadcasted_iota(jnp.int32, (256, 256), 0) < lax.broadcasted_iota(jnp.int32, (256, 256), 1)
    same = jnp.where((column == target) & before, 1, 0)
    rank = jnp.sum(same, axis=0, keepdims=True)
    dst = lax.broadcasted_iota(jnp.int32, (128, 256), 0)
    rows = [jnp.where((target == dst) & (rank == j), 1.0, 0.0) for j in range(2)]
    chosen = jnp.concatenate(rows, axis=0).astype(jnp.bfloat16)
    patch = jnp.where(sample == lax.broadcasted_iota(jnp.int32, (256, 256), 0), 1.0, 0.0).astype(jnp.bfloat16)
    return lax.dot_general(chosen, patch, (((1,), (1,)), ((), ())), preferred_element_type=jnp.float32).astype(jnp.bfloat16)

GATHER = ((0, 72), (72, 80), (152, 80))

def front_kernel(params, vel, visc, assign, sample, nxt, out, got, ext, vext, first, order, slots, s0, *rest):
    s1, s2, s3, relay = rest[0:3], rest[3:6], rest[6:9], rest[9:27]
    hs, hr, lsem, ssem, rsem, cs, cr, xs, xr, xl = rest[27:]
    xyz, core = coords()
    me = lax.axis_index("group") * 32 + lax.axis_index("dev")
    after, before = (me + 1) % 128, (me + 127) % 128
    after_id, before_id = (after // 32, after % 32), (before // 32, before % 32)
    block = (xyz[2] // 2, core, xyz[2] % 2, xyz[1], xyz[0])
    number = assign[...].astype(jnp.float32)
    slots[...] = jnp.zeros((8, 128), jnp.float32)
    slots[0:1] = number[:, :128]
    slots[1:2] = number[:, 128:]
    own = [pltpu.make_async_copy(params, out.at[block + (pl.ds(0, 224),)], lsem.at[0]),
           pltpu.make_async_copy(slots, out.at[block + (pl.ds(224, 8),)], lsem.at[1])]
    for c in own: c.start()
    barrier = pltpu.get_barrier_semaphore()
    ids = neighbours(xyz, core) + [ident(shifted(xyz, a, 2), core) for a in range(3)] + [after_id, before_id]
    for i in ids:
        pl.semaphore_signal(barrier, inc=1, device_id=i, device_id_type=MESH)
    ext[:, 2:10] = vel[...]
    vext[1:9] = visc[...]
    pl.semaphore_wait(barrier, len(ids))
    sib = ident(xyz, 1 - core)
    pend = []

    def remote(src, dst, s, r, to):
        c = pltpu.make_async_remote_copy(src_ref=src, dst_ref=dst, send_sem=s, recv_sem=r, device_id=to, device_id_type=MESH)
        c.start(); pend.append(c)
        return c

    sibs = []
    def to_sib(src):
        k = len(sibs)
        sibs.append(remote(src, src, cs.at[k], cr.at[k], sib))
    steps = {}
    def around(p, phase):
        a = ORDERS[p][phase]; full = ORDERS[p][:phase]
        at = [shifted(xyz, a, k) for k in range(4)]
        return full, at, ident(at[1], core), ident(at[3], core), halves(p, GATHER), (phase * 3 + p) * 6, GATHER[p]
    def g_send(p, phase, kind, at, half, to):
        full, _, _, _, hs_, base, _ = around(p, phase)
        r0, n = hs_[half]
        src = region(out, full, at, core, r0, n)
        steps[p, phase, kind] = remote(src, src, ssem.at[base + kind], rsem.at[base + kind], to)
    def g_start(phase):
        for p in range(3):
            full, at, R, L, hv, base, (r0, n) = around(p, phase)
            if phase == 0:
                src = region(out, full, at[0], core, r0, n)
                for kind, k in ((2, 2), (0, 1), (3, 3)):
                    steps[p, 0, kind] = remote(src, src, ssem.at[base + kind], rsem.at[base + kind], ident(at[k], core))
                continue
            g_send(p, phase, 0, at[0], 0, R)
            g_send(p, phase, 3, at[0], 1, L)
            g_send(p, phase, 1, at[0], 1, R)
            g_send(p, phase, 4, at[0], 0, L)
            if phase == 2: to_sib(region(out, full, at[0], core, r0, n))
    def g_forward(phase):
        for p in range(3):
            full, at, R, L, hv, base, _ = around(p, phase)
            steps[p, phase, 0].wait_recv(); g_send(p, phase, 2, at[3], 0, R)
            steps[p, phase, 3].wait_recv(); g_send(p, phase, 5, at[1], 1, L)
    def g_near(phase):
        for p in range(3):
            full, at, R, L, hv, base, (r0, n) = around(p, phase)
            steps[p, phase, 1].wait_recv(); steps[p, phase, 4].wait_recv()
            if phase == 2:
                to_sib(region(out, full, at[3], core, r0, n))
                to_sib(region(out, full, at[1], core, r0, n))
    def g_far(phase):
        for p in range(3):
            full, at, R, L, hv, base, (r0, n) = around(p, phase)
            steps[p, phase, 2].wait_recv(); steps[p, phase, 5].wait_recv()
            if phase == 2: to_sib(region(out, full, at[2], core, r0, n))

    moves, selfs = {}, {}
    def x_core():
        blocks = s0.reshape(3, 2, 2, 2, 4, 4, 16, 128)
        for p in range(3):
            for zh in range(2):
                k = p * 2 + zh
                moves[p, 0, zh] = remote(blocks.at[p, zh, 1 - core], s1[p].at[core, zh], xs.at[k], xr.at[k], sib)
                selfs[p, 0, zh] = pltpu.make_async_copy(blocks.at[p, zh, core], s1[p].at[core, zh], xl.at[k])
                selfs[p, 0, zh].start()
    def stage(p, s):
        a = ORDERS[p][s - 1]; others = ORDERS[p][s:]
        src = (s1, s2, s3)[s - 1][p]
        dst = got.at[p] if s == 3 else (s2, s3)[s - 1][p]
        at = [shifted(xyz, a, k) for k in range(4)]
        ahead = (slice(None),) * (s - 1)
        def part(k, sc): return src.at[ahead + (sc,) + pick(others, at[k], (a,) + others)]
        def land(k, sc): return dst.at[(at[k][a],) + ahead + (sc,)]
        return part, land, ident(at[1], core), ident(at[3], core), 6 + ((s - 1) * 3 + p) * 6
    def x_start(s):
        for p in range(3):
            part, land, R, L, base = stage(p, s)
            if s == 1:
                for zh in range(2): moves[p, 0, zh].wait_recv(); selfs[p, 0, zh].wait()
            else:
                for k in (0, 1, 4, 5): moves[p, s - 1, k].wait_recv()
                selfs[p, s - 1].wait()
            every = slice(None)
            def mv(k, src, dst, to): moves[p, s, k] = remote(src, dst, xs.at[base + k], xr.at[base + k], to)
            via = relay[((s - 1) * 3 + p) * 2], relay[((s - 1) * 3 + p) * 2 + 1]
            mv(2, part(2, 0), via[0], R)
            mv(3, part(2, 1), via[1], L)
            mv(0, part(1, every), land(0, every), R)
            mv(1, part(3, every), land(0, every), L)
            c = pltpu.make_async_copy(part(0, every), land(0, every), xl.at[6 + (s - 1) * 3 + p])
            c.start(); selfs[p, s] = c
    def x_relay(s):
        for p in range(3):
            part, land, R, L, base = stage(p, s)
            via = relay[((s - 1) * 3 + p) * 2], relay[((s - 1) * 3 + p) * 2 + 1]
            moves[p, s, 2].wait_recv()
            moves[p, s, 4] = remote(via[0], land(3, 0), xs.at[base + 4], xr.at[base + 4], R)
            moves[p, s, 3].wait_recv()
            moves[p, s, 5] = remote(via[1], land(1, 1), xs.at[base + 5], xr.at[base + 5], L)
    def x_finish():
        for p in range(3):
            for k in (0, 1, 4, 5): moves[p, 3, k].wait_recv()
            selfs[p, 3].wait()

    def put_first(x, new):
        for c in range(3): first[c, x] = new[c]
    def put_next(x, new):
        for c in range(3): nxt[c, x] = new[c]
    for c in own: c.wait()
    g_start(0)
    halo = [remote(vel.at[:, 6:8], ext.at[:, 0:2], hs.at[0], hr.at[0], after_id),
            remote(vel.at[:, 0:2], ext.at[:, 10:12], hs.at[1], hr.at[1], before_id),
            remote(visc.at[7:8], vext.at[0:1], hs.at[2], hr.at[2], after_id),
            remote(visc.at[0:1], vext.at[9:10], hs.at[3], hr.at[3], before_id)]
    order[...] = send_order(assign[...], sample[...])
    advance_planes(ext, vext, 2, 8, put_first)
    for p in range(3):
        for kind in (0, 2, 3): steps[p, 0, kind].wait_recv()
    g_start(1)
    for c in halo: c.wait_recv()
    lower = jnp.where(me > 0, 1.0, 0.0); upper = jnp.where(me < 127, 1.0, 0.0)
    ext[:, 0:2] = ext[:, 0:2] * lower
    vext[0:1] = vext[0:1] * lower
    ext[:, 10:12] = ext[:, 10:12] * upper
    vext[9:10] = vext[9:10] * upper
    advance_planes(ext, vext, 0, 2, put_first)
    advance_planes(ext, vext, 8, 10, put_first)
    g_forward(1)
    advance_planes(first, visc, 0, 8, put_next)
    g_near(1); g_far(1)
    g_start(2)
    def body(i, carry):
        c, q = i // 4, i % 4
        for field, ref, off in ((0, first, 1), (1, nxt, 0)):
            a, b = ref[c, 2 * q + off], ref[c, 2 * q + off + 1]
            pieces = []
            for iy in range(16):
                pieces += [a[iy * 8:iy * 8 + 8], b[iy * 8:iy * 8 + 8]]
            res = permuted(order[...], swap_groups(jnp.concatenate(pieces, axis=0)))
            for j in range(2):
                col = j * 24 + field * 12 + i
                s0[pl.ds((col // 16) * 2048 + col % 16, 128, stride=16), :] = res[j * 128:(j + 1) * 128]
        return carry
    lax.fori_loop(0, 12, body, 0)
    x_core()
    g_forward(2)
    x_start(1)
    g_near(2)
    x_relay(1)
    x_start(2)
    g_far(2)
    x_relay(2)
    x_start(3)
    x_relay(3)
    x_finish()
    for c in sibs: c.wait_recv()
    for c in pend: c.wait_send()

def front(params, vel, visc, assign, sample):
    f32, V = jnp.float32, pltpu.VMEM
    scratch = [V((3, 12, 128, 128), f32), V((10, 128, 128), f32), V((3, 10, 128, 128), f32), V((256, 256), jnp.bfloat16), V((8, 128), f32), V((6144, 128), f32)]
    scratch += [V((2, 2, 2, 4, 4, 16, 128), f32)] * 3
    for s in (2, 3):
        for p in range(3):
            scratch.append(V((4,) * (s - 1) + (2,) + dims(ORDERS[p][s - 1:]) + (16, 128), f32))
    for s in (1, 2, 3):
        for p in range(3):
            scratch += [V((4,) * (s - 1) + dims(ORDERS[p][s:]) + (16, 128), f32)] * 2
    D = pltpu.SemaphoreType.DMA
    scratch += [D((4,)), D((4,)), D((2,)), D((54,)), D((54,)), D((12,)), D((12,)), D((60,)), D((60,)), D((15,))]
    A = pl.BlockSpec(memory_space=pl.ANY); M = pl.BlockSpec(memory_space=pltpu.VMEM)
    return pl.pallas_call(
        front_kernel,
        out_shape=(jax.ShapeDtypeStruct((3, 8, 128, 128), f32), jax.ShapeDtypeStruct((2, 2, 2, 4, 4, 232, 128), f32),
                   jax.ShapeDtypeStruct((3, 4, 4, 4, 2, 16, 128), f32)),
        in_specs=[A, M, M, M, M], out_specs=(M, A, A), scratch_shapes=scratch,
        compiler_params=pltpu.CompilerParams(collective_id=0, has_side_effects=True, vmem_limit_bytes=58 << 20),
        name="front",
    )(params, vel, visc, assign, sample)

BLOCK = 232
WIN, WUP, WDN, WOUT = (0, 1536, 4), (6144, 512, 16), (14336, 2048, 4), (22528, 512, 12)
NN = (((1,), (0,)), ((), ())); NT = (((1,), (1,)), ((), ()))

def split2(x):
    high = x.astype(jnp.bfloat16)
    return high, (x - high.astype(jnp.float32)).astype(jnp.bfloat16)

def dot3(a, b, form):
    d = lambda p, q: lax.dot_general(p, q, form, preferred_element_type=jnp.float32)
    return d(a[0], b[0]) + (d(a[0], b[1]) + d(a[1], b[0]))

def put2(refs, value, *at):
    for r, v in zip(refs, split2(value)): r[at] = v

def unpack(flat, spec, hi, lo):
    base, rows, cols = spec
    n = 256
    def body(i, carry):
        for q in range(cols):
            start = base + i * (n * cols) + q
            h, l = split2(flat[pl.ds(start, n, stride=cols), :])
            at = (pl.ds(pl.multiple_of(i * n, n), n), pl.ds(q * 128, 128))
            hi[at] = h; lo[at] = l
        return carry
    lax.fori_loop(0, rows // n, body, 0)

def pack(flat, spec, r0, n, c0, value):
    base, rows, cols = spec
    for q in range(value.shape[1] // 128):
        flat[pl.ds(base + r0 * cols + c0 + q, n, stride=cols), :] = value[:, q * 128:(q + 1) * 128]

def slot_matrices(assign, me):
    mine = (assign // 256) == me
    t = lax.broadcasted_iota(jnp.int32, (128, 256), 1)
    first = jnp.min(jnp.where(mine, t, 512), axis=1, keepdims=True)
    last = jnp.max(jnp.where(mine, t, -1), axis=1, keepdims=True)
    slot = assign % 256
    cols = [jnp.sum(jnp.where(t == at, slot, 0), axis=1, keepdims=True) for at in (first, last)]
    want = [jnp.where(c == t, 1.0, 0.0).astype(jnp.bfloat16) for c in cols]
    k = lax.broadcasted_iota(jnp.int32, (128, 128), 0)
    src = lax.broadcasted_iota(jnp.int32, (128, 128), 1)
    moved = []
    for p in range(3):
        co = {ORDERS[p][2]: k // 32, ORDERS[p][1]: (k // 8) % 4, ORDERS[p][0]: (k // 2) % 4}
        flat = (co[2] // 2) * 64 + (k % 2) * 32 + (co[2] % 2) * 16 + co[1] * 4 + co[0]
        perm = jnp.where(flat == src, 1.0, 0.0).astype(jnp.bfloat16)
        moved.append([jnp.dot(perm, w, preferred_element_type=jnp.float32) for w in want])
    return [jnp.transpose(jnp.concatenate([moved[p0][0], moved[p1][1]], axis=0)).astype(jnp.bfloat16) for p0, p1 in PAIRS]

PAIRS = ((0, 1), (0, 2), (1, 2))

def back_kernel(got, gathered, pred, mine, flat, asg, win, winl, wup, wupl, wdn, wdnl, wout, woutl,
                 x, tgt, xs, xsl, hid, pre, a5, a5l, state, state2, rowsc, crecv, *rest):
    bufs, (sem, cs, cr, ssem, rsem) = rest[:33], rest[33:]
    me = lax.axis_index("group") * 32 + lax.axis_index("dev")
    xyz, core = coords()
    barrier = pltpu.get_barrier_semaphore()
    ids = neighbours(xyz, core) + [ident(shifted(xyz, a, 2), core) for a in range(3)]
    for i in ids:
        pl.semaphore_signal(barrier, inc=1, device_id=i, device_id_type=MESH)
    ac = pltpu.make_async_copy(gathered.at[:, pl.ds(224, 8), :], asg, sem.at[0])
    wc = pltpu.make_async_copy(gathered.at[:, pl.ds(0, 224), :], flat.reshape(128, 224, 128), sem.at[1])
    ac.start(); wc.start()
    ac.wait()
    assign = jnp.concatenate([asg[:, 0, :], asg[:, 1, :]], axis=1).astype(jnp.int32)
    for i, place in enumerate(slot_matrices(assign, me)): rowsc[i] = place
    for field, ref in ((0, x), (1, tgt)):
        for k in range(12):
            col = [j * 24 + field * 12 + k for j in range(2)]
            src = jnp.concatenate([got[pl.ds((c // 16) * 2048 + c % 16, 128, stride=16), :] for c in col], axis=0)
            ref[:, k * 128:(k + 1) * 128] = permuted(rowsc[(col[0]) // 8], src)
    wc.wait()
    unpack(flat, WIN, win, winl)
    unpack(flat, WUP, wup, wupl)
    unpack(flat, WDN, wdn, wdnl)
    unpack(flat, WOUT, wout, woutl)
    put2((xs, xsl), x[...], slice(None), slice(None))
    state[...] = dot3((xs[...], xsl[...]), (win[...], winl[...]), NN)
    s = state[...]
    r = lax.rsqrt(jnp.mean(s * s, axis=1, keepdims=True) + norm_epsilon)
    put2((a5, a5l), s * r, slice(None), slice(None))
    c1, c2 = 0.7978845608028654, 0.044715
    def up(n, carry):
        at = (slice(None), pl.ds(pl.multiple_of(n * 1024, 1024), 1024))
        p = dot3((a5[...], a5l[...]), (wup[at], wupl[at]), NN)
        th = jnp.tanh(c1 * (p + c2 * (p * p * p)))
        pre[at] = 0.5 * (1.0 + th) + 0.5 * p * (1.0 - th * th) * (c1 * (1.0 + (3.0 * c2) * (p * p)))
        hid[at] = 0.5 * p * (1.0 + th)
        return carry
    lax.fori_loop(0, 2, up, 0)
    def down(n, acc):
        at = (slice(None), pl.ds(pl.multiple_of(n * 1024, 1024), 1024))
        wat = (pl.ds(pl.multiple_of(n * 1024, 1024), 1024), slice(None))
        return acc + dot3(split2(hid[at]), (wdn[wat], wdnl[wat]), NN)
    state2[...] = lax.fori_loop(0, 2, down, s)
    s2 = split2(state2[...])
    def outp(n, carry):
        at = (slice(None), pl.ds(pl.multiple_of(n * 768, 768), 768))
        g = x[at] + dot3(s2, (wout[at], woutl[at]), NN)
        pred[at] = g
        tgt[at] = (g - tgt[at]) * (1.0 / 256.0)
        return carry
    lax.fori_loop(0, 2, outp, 0)
    blocks = flat.reshape(2, 2, 2, 4, 4, 224, 128)
    sib = ident(xyz, 1 - core)
    def swap(n):
        src, dst = (blocks.at[1, 1 - core], crecv.at[1]) if n == 0 else (blocks.at[0, 1 - core, n - 1], crecv.at[0, n - 1])
        return pltpu.make_async_remote_copy(src_ref=src, dst_ref=dst, send_sem=cs.at[n], recv_sem=cr.at[n], device_id=sib, device_id_type=MESH)
    def swap_add(n):
        swap(n).wait_recv()
        def body(i, carry):
            at = ((1, i // 16) if n == 0 else (0, n - 1)) + ((i // 4) % 4, i % 4)
            mineat = (at[0], core) + at[1:]
            blocks[mineat] = blocks[mineat] + crecv[at]
            return carry
        lax.fori_loop(0, 32 if n == 0 else 16, body, 0)
    s2t = split2(jnp.transpose(state2[...]))
    def gout(n, acc):
        at = (slice(None), pl.ds(pl.multiple_of(n * 768, 768), 768))
        e = split2(tgt[at])
        pack(flat, WOUT, 0, 512, n * 6, dot3(s2t, e, NN))
        return acc + dot3(e, (wout[at], woutl[at]), NT)
    ds2 = lax.fori_loop(0, 2, gout, jnp.zeros((256, 512), jnp.float32))
    state2[...] = ds2
    put2((xs, xsl), ds2, slice(None), pl.ds(0, 512))
    dss = lambda: (xs[:, :512], xsl[:, :512])
    normt = jnp.transpose(state[...] * r)
    nt = split2(normt)
    def gdown(n, carry):
        at = (slice(None), pl.ds(pl.multiple_of(n * 1024, 1024), 1024))
        pack(flat, WDN, n * 1024, 1024, 0, dot3(split2(jnp.transpose(hid[at])), dss(), NN))
        return carry
    lax.fori_loop(0, 2, gdown, 0)
    pl.semaphore_wait(barrier, len(ids))
    swap(0).start()
    def hidden(n, acc):
        at = (slice(None), pl.ds(pl.multiple_of(n * 512, 512), 512))
        wat = (pl.ds(pl.multiple_of(n * 512, 512), 512), slice(None))
        dh = dot3(dss(), (wdn[wat], wdnl[wat]), NT)
        dps = split2(dh * pre[at])
        pack(flat, WUP, 0, 512, n * 4, dot3(nt, dps, NN))
        return acc + dot3(dps, (wup[at], wupl[at]), NT)
    pend = []
    first, second, third = big_phase(blocks, bufs, ssem, rsem, xyz, core, pend)
    lower, upper = (0, 1, 2), (3, 4)
    dn = lax.fori_loop(0, 2, hidden, jnp.zeros((256, 512), jnp.float32))
    swap_add(0)
    first(upper)
    dn = lax.fori_loop(2, 4, hidden, dn)
    @pl.when(core == 0)
    def _():
        swap(1).start()
        swap(2).start()
    second(upper)
    norm = state[...] * r
    ds = state2[...] + r * (dn - norm * jnp.mean(dn * norm, axis=1, keepdims=True))
    put2((a5, a5l), ds, slice(None), slice(None))
    def gin(n, carry):
        at = (slice(None), pl.ds(pl.multiple_of(n * 512, 512), 512))
        pack(flat, WIN, n * 512, 512, 0, dot3(split2(jnp.transpose(x[at])), (a5[...], a5l[...]), NN))
        return carry
    lax.fori_loop(0, 2, gin, 0)
    @pl.when(core == 1)
    def _(): swap(1).start()
    lax.fori_loop(2, 3, gin, 0)
    @pl.when(core == 1)
    def _(): swap(2).start()
    swap_add(1)
    swap_add(2)
    first(lower)
    third(upper)
    second(lower)
    third(lower)
    small_phases(blocks, mine, bufs[12:], ssem, rsem, xyz, core, pend)
    for c in pend: c.wait_send()
    for n in range(3): swap(n).wait_send()

SPREAD = ((0, 48), (48, 88), (136, 88))
UNITS = ((0, None), (1, 0), (2, 0), (1, 1), (2, 1))

def place(full, at, core, r0, n, half=None):
    i = pick(full, at)
    if half is not None: i = (half,) + i[1:]
    return (i[0], core) + i[1:] + (pl.ds(r0, n), slice(None))

def walk_half(full, xyz, half, body):
    sizes = [2 if a == 2 and half is not None else 4 for a in full]
    count = 1
    for n in sizes: count *= n
    def step(i, carry):
        at = list(xyz)
        for a, n in zip(full, sizes):
            at[a] = i % n + (2 * half if n == 2 else 0)
            i = i // n
        body(tuple(at)); return carry
    lax.fori_loop(0, count, step, 0)

def big_phase(blocks, bufs, ssem, rsem, xyz, core, pend):
    copies = {}
    def of(u):
        p, half = UNITS[u]; a = ORDERS[p][2]; full = ORDERS[p][:2]
        ids = [ident(shifted(xyz, a, k), core) for k in range(4)]
        refs = [b if half is None else b.at[half] for b in bufs[p * 4:p * 4 + 4]]
        lead = (slice(None),) * (len(dims(full)) - (half is not None))
        return p, half, a, full, ids, refs, lead
    def send(u, kind, rel, r0, n, to, dst):
        p, half, a, full, ids, _, _ = of(u)
        c = pltpu.make_async_remote_copy(src_ref=blocks.at[place(full, shifted(xyz, a, rel), core, r0, n, half)], dst_ref=dst,
            send_sem=ssem.at[u * 6 + kind], recv_sem=rsem.at[u * 6 + kind], device_id=ids[to], device_id_type=MESH)
        c.start(); copies[u, kind] = c; pend.append(c)
    def fold(u, kind, rel, r0, n, slot, off):
        p, half, a, full, _, _, _ = of(u)
        copies[u, kind].wait_recv()
        ref = bufs[p * 4 + slot]
        def body(at):
            i = place((), at, core, r0, n)
            blocks[i] = blocks[i] + ref[pick((), at, full) + (pl.ds(off, n), slice(None))]
        walk_half(full, shifted(xyz, a, rel), half, body)
    def first(units):
        for u in units:
            p, _, _, _, _, refs, lead = of(u)
            (h0, n0), (h1, n1) = halves(p, SPREAD)
            send(u, 0, 2, h0, n0, 1, refs[0])
            send(u, 3, 2, h1, n1, 3, refs[1])
        for u in units:
            p, _, _, _, _, refs, lead = of(u)
            (h0, n0), (h1, n1) = halves(p, SPREAD)
            send(u, 1, 1, h1, n1, 1, refs[2].at[lead + (pl.ds(n0, n1),)])
            send(u, 4, 3, h0, n0, 3, refs[3].at[lead + (pl.ds(0, n0),)])
    def second(units):
        for u in units:
            p, _, _, _, _, refs, lead = of(u)
            (h0, n0), (h1, n1) = halves(p, SPREAD)
            fold(u, 0, 1, h0, n0, 0, 0); send(u, 2, 1, h0, n0, 1, refs[2].at[lead + (pl.ds(0, n0),)])
            fold(u, 3, 3, h1, n1, 1, 0); send(u, 5, 3, h1, n1, 3, refs[3].at[lead + (pl.ds(n0, n1),)])
    def third(units):
        for u in units:
            (h0, n0), (h1, n1) = halves(UNITS[u][0], SPREAD)
            fold(u, 1, 0, h1, n1, 2, n0); fold(u, 4, 0, h0, n0, 3, 0)
        for u in units:
            (h0, n0), (h1, n1) = halves(UNITS[u][0], SPREAD)
            fold(u, 2, 0, h0, n0, 2, 0); fold(u, 5, 0, h1, n1, 3, n0)
    return first, second, third

def small_phases(blocks, mine, bufs, ssem, rsem, xyz, core, pend):
    copies = {}
    def send(p, phase, kind, rel, r0, n, to, dst):
        a = ORDERS[p][2 - phase]; full = ORDERS[p][:2 - phase]
        k = 30 + ((phase - 1) * 3 + p) * 6 + kind
        c = pltpu.make_async_remote_copy(src_ref=blocks.at[place(full, shifted(xyz, a, rel), core, r0, n)], dst_ref=dst,
            send_sem=ssem.at[k], recv_sem=rsem.at[k], device_id=ident(shifted(xyz, a, to), core), device_id_type=MESH)
        c.start(); copies[p, phase, kind] = c; pend.append(c)
    def fold(p, phase, kind, rel, r0, n, ref, off):
        a = ORDERS[p][2 - phase]; full = ORDERS[p][:2 - phase]
        copies[p, phase, kind].wait_recv()
        def body(at):
            i = place((), at, core, r0, n)
            blocks[i] = blocks[i] + ref[pick((), at, full) + (pl.ds(off, n), slice(None))]
        walk(full, shifted(xyz, a, rel), body)
    for p in range(3):
        b = bufs[p * 4:p * 4 + 4]; (h0, n0), (h1, n1) = halves(p, SPREAD)
        lead = (slice(None),) * len(dims(ORDERS[p][:1]))
        send(p, 1, 0, 2, h0, n0, 1, b[0])
        send(p, 1, 3, 2, h1, n1, 3, b[1])
        send(p, 1, 1, 1, h1, n1, 1, b[2].at[lead + (pl.ds(n0, n1),)])
        send(p, 1, 4, 3, h0, n0, 3, b[3].at[lead + (pl.ds(0, n0),)])
    for p in range(3):
        b = bufs[p * 4:p * 4 + 4]; (h0, n0), (h1, n1) = halves(p, SPREAD)
        lead = (slice(None),) * len(dims(ORDERS[p][:1]))
        fold(p, 1, 0, 1, h0, n0, b[0], 0); send(p, 1, 2, 1, h0, n0, 1, b[2].at[lead + (pl.ds(0, n0),)])
        fold(p, 1, 3, 3, h1, n1, b[1], 0); send(p, 1, 5, 3, h1, n1, 3, b[3].at[lead + (pl.ds(n0, n1),)])
    for p in range(3):
        b = bufs[p * 4:p * 4 + 4]; (h0, n0), (h1, n1) = halves(p, SPREAD)
        fold(p, 1, 1, 0, h1, n1, b[2], n0); fold(p, 1, 4, 0, h0, n0, b[3], 0)
    for p in range(3):
        b = bufs[p * 4:p * 4 + 4]; (h0, n0), (h1, n1) = halves(p, SPREAD)
        fold(p, 1, 2, 0, h0, n0, b[2], 0); fold(p, 1, 5, 0, h1, n1, b[3], n0)
        b = bufs[12 + p * 3:15 + p * 3]; r0, n = SPREAD[p]
        send(p, 2, 0, 2, r0, n, 2, b[2])
        send(p, 2, 1, 1, r0, n, 1, b[0])
        send(p, 2, 2, 3, r0, n, 3, b[1])
    for p in range(3):
        b = bufs[12 + p * 3:15 + p * 3]; r0, n = SPREAD[p]
        fold(p, 2, 0, 0, r0, n, b[2], 0); fold(p, 2, 1, 0, r0, n, b[0], 0); fold(p, 2, 2, 0, r0, n, b[1], 0)
    mine[...] = blocks[(xyz[2] // 2, core, xyz[2] % 2, xyz[1], xyz[0])]

def back(got, gathered):
    f32, b16 = jnp.float32, jnp.bfloat16
    V = pltpu.VMEM
    both = lambda *s: [V(s, b16), V(s, b16)]
    slots = []
    for phase in range(2):
        for p in range(3):
            lead = dims(ORDERS[p][:2 - phase]); (_, n0), (_, n1) = halves(p, SPREAD)
            slots += [V(lead + (n, 128), f32) for n in (n0, n1, n0 + n1, n0 + n1)]
    for p in range(3): slots += [V((SPREAD[p][1], 128), f32)] * 3
    return pl.pallas_call(
        back_kernel,
        out_shape=(jax.ShapeDtypeStruct((256, 1536), f32), jax.ShapeDtypeStruct((224, 128), f32)),
        in_specs=[pl.BlockSpec(memory_space=pltpu.VMEM), pl.BlockSpec(memory_space=pl.ANY)],
        out_specs=(pl.BlockSpec(memory_space=pltpu.VMEM), pl.BlockSpec(memory_space=pltpu.VMEM)),
        scratch_shapes=[V((28672, 128), f32), V((128, 8, 128), f32)] + both(1536, 512) + both(512, 2048) + both(2048, 512) + both(512, 1536)
            + [V((256, 1536), f32), V((256, 1536), f32)] + both(256, 1536) + [V((256, 2048), f32), V((256, 2048), f32)] + both(256, 512)
            + [V((256, 512), f32), V((256, 512), f32), V((3, 256, 256), b16), V((2, 2, 4, 4, 224, 128), f32)] + slots
            + [pltpu.SemaphoreType.DMA((n,)) for n in (2, 3, 3, 66, 66)],
        compiler_params=pltpu.CompilerParams(collective_id=1, has_side_effects=True, vmem_limit_bytes=61 << 20),
        name="back",
    )(got, gathered)

def adam(shard, grad, moment, second):
    new_m = beta_first * moment + (1.0 - beta_first) * grad
    new_v = beta_second * second + (1.0 - beta_second) * grad * grad
    update = (
        new_m
        / (1.0 - beta_first**adam_count)
        / (jnp.sqrt(new_v / (1.0 - beta_second**adam_count)) + adam_epsilon)
    )
    return (shard - learn_rate * update, new_m, new_v)

def finish_kernel(nxt, pred, grad, shard, moment, second, nxt_out, pred_out, shard_out, moment_out, second_out, sems):
    copies = [pltpu.make_async_copy(nxt.at[c], nxt_out.at[c], sems.at[c]) for c in range(3)]
    copies += [pltpu.make_async_copy(pred.at[pl.ds(64 * i, 64)], pred_out.at[pl.ds(64 * i, 64)], sems.at[3 + i]) for i in range(4)]
    for c in copies: c.start()
    shard_out[...], moment_out[...], second_out[...] = adam(shard[...], grad[...], moment[...], second[...])
    for c in copies: c.wait()

def finish(nxt, pred, *rest):
    A = pl.BlockSpec(memory_space=pl.ANY); M = pl.BlockSpec(memory_space=pltpu.VMEM)
    return pl.pallas_call(
        finish_kernel,
        out_shape=[jax.ShapeDtypeStruct(a.shape, jnp.float32) for a in (nxt, pred) + rest[:3]],
        in_specs=[A, A, M, M, M, M], out_specs=[A, A, M, M, M],
        scratch_shapes=[pltpu.SemaphoreType.DMA((7,))],
        compiler_params=pltpu.CompilerParams(vmem_limit_bytes=60 << 20),
        name="finish",
    )(nxt, pred, *rest)

def local(velocity, viscosity, sample_idx, assign, params, adam_m, adam_v):
    velocity_next, gathered, got = front(params.reshape(224, 128), velocity, viscosity, assign, sample_idx)
    prediction, grad = back(got.reshape(6144, 128), gathered.reshape(128, 232, 128))
    velocity_next, prediction, *new = finish(velocity_next, prediction, grad, *[a.reshape(224, 128) for a in (params, adam_m, adam_v)])
    return (velocity_next, prediction, *[a.reshape(-1) for a in new])


def solution(mesh):
    placed = (
        P(None, ("group", "dev"), None, None),
        P(("group", "dev"), None, None),
        P(("group", "dev"), None),
        P(("group", "dev"), None),
        P(("group", "dev")),
        P(("group", "dev")),
        P(("group", "dev")),
    )
    return jax.shard_map(
        local,
        mesh=mesh,
        in_specs=placed,
        out_specs=(
            P(None, ("group", "dev"), None, None),
            P(("group", "dev"), None),
            P(("group", "dev")),
            P(("group", "dev")),
            P(("group", "dev")),
        ),
        check_vma=False,
    )
```
